32 devices in a mesh: region: 16 (over z, x, core), event: 2 (over y).
Axes of the slice: x: 2, y: 2, z: 4, core: 2. Of those that a mesh axis runs over, the one named last changes fastest.
Arguments:
- forward_field: float32 [2, 3, 128, 9, 128], P('event', None, 'region'), may hold values from -6 to 6
- forward_speed: float32 [2, 3, 128, 9, 128], P('event', None, 'region'), may hold values from -6 to 6
- adjoint_field: float32 [2, 3, 128, 9, 128], P('event', None, 'region'), may hold values from -6 to 6
- adjoint_speed: float32 [2, 3, 128, 9, 128], P('event', None, 'region'), may hold values from -6 to 6
- adjoint_source: float32 [2, 3, 128, 9, 128], P('event', None, 'region'), may hold values from -6 to 6
- lame_lambda: float32 [128, 9, 128], P('region'), may hold values from 0.5 to 2
- lame_mu: float32 [128, 9, 128], P('region'), may hold values from 0.3 to 1.2
- density: float32 [128, 9, 128], P('region'), may hold values from 0.8 to 2.4
Outputs:
- forward_out: float32 [2, 3, 128, 9, 128], P('event', None, 'region')
- forward_speed_out: float32 [2, 3, 128, 9, 128], P('event', None, 'region')
- adjoint_out: float32 [2, 3, 128, 9, 128], P('event', None, 'region')
- adjoint_speed_out: float32 [2, 3, 128, 9, 128], P('event', None, 'region')
- kernels: float32 [2, 128, 9, 128], P(None, ('region', 'event'))
The draws below stay inside these ranges and needn't reach their ends.
All inputs are finite; a program needn't handle non-finite values.
Results may differ from the reference program's by a relative error of at most 0.0003.
Values sent between devices are 32-bit elements; how exact they have to be, the bound alone decides.
A program may use at most 64 MiB of HBM per device.

```python
import math
import jax
import jax.numpy as jnp
import numpy as np
from jax import lax

STEPS = 2
EVENTS = 2
NXG = 128
NY = 128
NZ = 9


def steps_of(key, extent, pieces, least, high):
    loudness, own = 1.0, jax.random.fold_in(key, 6)
    for dim, shards_of in pieces:
        draws = jnp.exp(jax.random.uniform(jax.random.fold_in(own, dim), (shards_of,), jnp.float32, least / len(pieces), high / len(pieces)))
        loudness = loudness * jnp.repeat(draws, extent[dim] // shards_of).reshape([-1 if axis == dim else 1 for axis in range(len(extent))])
    return loudness


def centred(own_key, shape, deviation, limit, cuts=(), kind=jnp.bfloat16):
    level = steps_of(own_key, shape, cuts, -0.22, 0.18) if cuts else 1.0
    drawn = jax.random.normal(own_key, shape, jnp.float32) * deviation * level
    return jnp.minimum(jnp.maximum(drawn, -limit), limit).astype(kind)


def setup_inputs(seed: int = 0) -> dict:
    splits = jax.random.split(jax.random.key(seed), 9)
    forward_field = centred(splits[0], (EVENTS, 3, NXG, NZ, NY), 1.0, 6.0, ((0, 2), (2, 16)), jnp.float32)
    forward_speed = centred(splits[1], (EVENTS, 3, NXG, NZ, NY), 1.0, 6.0, ((0, 2), (2, 16)), jnp.float32)
    adjoint_field = centred(splits[2], (EVENTS, 3, NXG, NZ, NY), 1.0, 6.0, ((0, 2), (2, 16)), jnp.float32)
    adjoint_speed = centred(splits[3], (EVENTS, 3, NXG, NZ, NY), 1.0, 6.0, ((0, 2), (2, 16)), jnp.float32)
    adjoint_source = centred(splits[4], (EVENTS, 3, NXG, NZ, NY), 1.0, 6.0, ((0, 2), (2, 16)), jnp.float32)
    lame_lambda = jnp.clip(jnp.exp(math.log(2.0) - 1.3862944 * jax.random.uniform(splits[5], (NXG, NZ, NY), jnp.float32) ** steps_of(splits[5], (NXG, NZ, NY), ((0, 16),), -0.2, 0.2)), 0.5, 2.0)
    lame_mu = jnp.clip(jnp.exp(math.log(1.2) - 1.3862944 * jax.random.uniform(splits[6], (NXG, NZ, NY), jnp.float32) ** steps_of(splits[6], (NXG, NZ, NY), ((0, 16),), -0.2, 0.2)), 0.3, 1.2)
    density = jnp.clip(jnp.exp(math.log(2.4) - 1.0986123 * jax.random.uniform(splits[7], (NXG, NZ, NY), jnp.float32) ** steps_of(splits[7], (NXG, NZ, NY), ((0, 16),), -0.2, 0.2)), 0.8, 2.4)
    return {"forward_field": forward_field, "forward_speed": forward_speed, "adjoint_field": adjoint_field, "adjoint_speed": adjoint_speed, "adjoint_source": adjoint_source, "lame_lambda": lame_lambda, "lame_mu": lame_mu, "density": density}


time_step = 0.02

def gll_tables():
    points = np.array([-1.0, -math.sqrt(3.0 / 7.0), 0.0, math.sqrt(3.0 / 7.0), 1.0])
    weights = np.array([0.1, 49.0 / 90.0, 32.0 / 45.0, 49.0 / 90.0, 0.1])
    legendre = (35.0 * points ** 4 - 30.0 * points ** 2 + 3.0) / 8.0
    derivative = np.zeros((5, 5))
    for target in range(5):
        for column in range(5):
            if target != column:
                derivative[target, column] = legendre[target] / (legendre[column] * (points[target] - points[column]))
    derivative[0, 0] = -5.0
    derivative[4, 4] = 5.0
    return (jnp.asarray(derivative, jnp.float32), jnp.asarray(weights, jnp.float32))

def expand_axis(nodes, axis):
    moved = jnp.moveaxis(nodes, axis, 0)
    planes = (moved.shape[0] - 1) // 4
    trailing = moved.shape[1:]
    leading = moved[:4 * planes].reshape((planes, 4) + trailing)
    closing = moved[4:4 * planes + 1:4].reshape((planes, 1) + trailing)
    joined = jnp.concatenate([leading, closing], axis=1)
    return jnp.moveaxis(joined, (0, 1), (axis, axis + 1))

def collapse_axis(values, axis):
    moved = jnp.moveaxis(values, (axis, axis + 1), (0, 1))
    planes = moved.shape[0]
    trailing = moved.shape[2:]
    leading = moved[:, :4].reshape((4 * planes,) + trailing)
    padding = jnp.zeros((planes, 3) + trailing, moved.dtype)
    shifted = jnp.concatenate([moved[:, 4:5], padding], axis=1).reshape((4 * planes,) + trailing)
    upper = jnp.concatenate([leading, jnp.zeros((1,) + trailing, moved.dtype)], axis=0)
    lower = jnp.concatenate([jnp.zeros((4,) + trailing, moved.dtype), shifted[:4 * planes - 3]], axis=0)
    return jnp.moveaxis(upper + lower, 0, axis)

def to_elements(nodes, first):
    for offset in (0, 2, 4):
        nodes = expand_axis(nodes, first + offset)
    return nodes

def to_nodes(values, first):
    for offset in (4, 2, 0):
        values = collapse_axis(values, first + offset)
    return values

def element_work(forward_nodes, adjoint_nodes, lambda_nodes, mu_nodes):
    derivative, weights = gll_tables()
    quadrature = weights[None, :, None, None, None, None] * weights[None, None, None, :, None, None] * weights[None, None, None, None, None, :]
    lambda_values = to_elements(lambda_nodes, 0)
    mu_values = to_elements(mu_nodes, 0)
    highest = lax.Precision.HIGHEST
    forms = ('pi,xpyjzk->xiyjzk', 'pj,xiypzk->xiyjzk', 'pk,xiyjzp->xiyjzk')

    def strains(nodes):
        values = to_elements(nodes, 1)
        grads = (jnp.einsum('pi,cxiyjzk->cxpyjzk', derivative, values, precision=highest), jnp.einsum('pj,cxiyjzk->cxiypzk', derivative, values, precision=highest), jnp.einsum('pk,cxiyjzk->cxiyjzp', derivative, values, precision=highest))
        table = [[0.5 * (grads[source][target] + grads[target][source]) for target in range(3)] for source in range(3)]
        dilation = table[0][0] + table[1][1] + table[2][2]
        return (dilation, table)

    def forces(dilation, table):
        components = []
        for target in range(3):
            total = 0.0
            for source in range(3):
                stress = 2.0 * mu_values * table[source][target]
                if source == target:
                    stress = stress + lambda_values * dilation
                total = total + jnp.einsum(forms[source], derivative, quadrature * stress, precision=highest)
            components.append(total)
        return to_nodes(jnp.stack(components), 1)
    dilation_fwd, table_fwd = strains(forward_nodes)
    dilation_adj, table_adj = strains(adjoint_nodes)
    shear_sum = 0.0
    for source in range(3):
        for target in range(3):
            shear_sum = shear_sum + table_fwd[source][target] * table_adj[source][target]
    increments = jnp.stack([quadrature * dilation_fwd * dilation_adj, 2.0 * quadrature * shear_sum])
    return (forces(dilation_fwd, table_fwd), forces(dilation_adj, table_adj), to_nodes(increments, 1))

def line_weights(count, closed):
    positions = jnp.arange(count) % 4
    values = jnp.where(positions == 0, 0.2, jnp.where(positions == 2, 32.0 / 45.0, 49.0 / 90.0)).astype(jnp.float32)
    if closed:
        values = values.at[0].set(0.1).at[count - 1].set(0.1)
    return values

def mass_of(density):
    return density * line_weights(density.shape[0], False)[:, None, None] * line_weights(density.shape[1], True)[None, :, None] * line_weights(density.shape[2], False)[None, None, :]

def extend_both(nodes):
    with_first = jnp.concatenate([nodes, nodes[:, :1]], axis=1)
    return jnp.concatenate([with_first, with_first[..., :1]], axis=-1)

def extend_model(nodes):
    with_first = jnp.concatenate([nodes, nodes[:1]], axis=0)
    return jnp.concatenate([with_first, with_first[..., :1]], axis=-1)

def wrap_planes(values):
    lateral = values[..., :-1].at[..., 0].add(values[..., -1])
    return lateral[:, :-1].at[:, 0].add(lateral[:, -1])

def reference(forward_field, forward_speed, adjoint_field, adjoint_speed, adjoint_source, lame_lambda, lame_mu, density):
    node_mass = mass_of(density)
    lambda_nodes = extend_model(lame_lambda)
    mu_nodes = extend_model(lame_mu)

    def one_event(items):
        forward_now, forward_rate, adjoint_now, adjoint_rate, source = items
        kernel_total = jnp.zeros((2,) + forward_now.shape[1:], jnp.float32)
        for step_index in range(STEPS):
            forward_force, adjoint_force, increments = element_work(extend_both(forward_now), extend_both(adjoint_now), lambda_nodes, mu_nodes)
            forward_rate = forward_rate - time_step * wrap_planes(forward_force) / node_mass
            forward_now = forward_now + time_step * forward_rate
            adjoint_rate = adjoint_rate + time_step * (source - wrap_planes(adjoint_force)) / node_mass
            adjoint_now = adjoint_now + time_step * adjoint_rate
            kernel_total = kernel_total + wrap_planes(increments)
        return (forward_now, forward_rate, adjoint_now, adjoint_rate, kernel_total)
    results = lax.map(one_event, (forward_field, forward_speed, adjoint_field, adjoint_speed, adjoint_source))
    return (results[0], results[1], results[2], results[3], lax.optimization_barrier(jnp.sum(results[4], axis=0)))
```

```python
import functools
import math

import jax
import jax.numpy as jnp
import numpy as np
from jax import lax
from jax.experimental import pallas as pl
from jax.experimental.pallas import tpu as pltpu
from jax.sharding import PartitionSpec as P

STEPS = 2
time_step = 0.02
MESH = pl.DeviceIdType.MESH


def gll_numbers():
    points = np.array([-1.0, -math.sqrt(3.0 / 7.0), 0.0, math.sqrt(3.0 / 7.0), 1.0])
    weights = np.array([0.1, 49.0 / 90.0, 32.0 / 45.0, 49.0 / 90.0, 0.1])
    legendre = (35.0 * points**4 - 30.0 * points**2 + 3.0) / 8.0
    derivative = np.zeros((5, 5))
    for target in range(5):
        for column in range(5):
            if target != column:
                derivative[target, column] = legendre[target] / (
                    legendre[column] * (points[target] - points[column])
                )
    derivative[0, 0] = -5.0
    derivative[4, 4] = 5.0
    return (derivative, weights)


def lane_tables(lanes):
    numbers, _ = gll_numbers()
    table = np.zeros((lanes, 2 * lanes))
    for lane in range(lanes):
        start, local = lane - lane % 4, lane % 4
        for source in range(5):
            if local:
                table[(start + source) % lanes, lane] += numbers[local, source]
            else:
                right, left = (start + source) % lanes, (start - 4 + source) % lanes
                table[right, lane] += 0.5 * numbers[0, source]
                table[left, lane] += 0.5 * numbers[4, source]
                table[right, lanes + lane] += 0.5 * numbers[0, source]
                table[left, lanes + lane] -= 0.5 * numbers[4, source]
    high = table.astype(np.float32).astype(jnp.bfloat16)
    low = (table - high.astype(np.float64)).astype(np.float32).astype(jnp.bfloat16)
    return (
        np.concatenate([high, high], axis=0),
        low,
        np.concatenate([high.T, low.T], axis=1),
        np.ascontiguousarray(high.T),
    )


def combine(coefficients, pieces):
    total = None
    for number, piece in zip(coefficients, pieces):
        if number != 0.0:
            term = float(number) * piece
            total = term if total is None else total + term
    return total


def turn(value, shift):
    return pltpu.roll(value, shift % 8, value.ndim - 2)


def row_bit(shape, bit):
    return (lax.broadcasted_iota(jnp.int32, shape, len(shape) - 2) & bit) == 0


def swap_rows(four):
    shape = four[0].shape
    low_two, low_one = row_bit(shape, 2), row_bit(shape, 1)
    a0, a1, a2, a3 = four
    b0 = jnp.where(low_two, a0, turn(a2, 2))
    b2 = jnp.where(low_two, turn(a0, -2), a2)
    b1 = jnp.where(low_two, a1, turn(a3, 2))
    b3 = jnp.where(low_two, turn(a1, -2), a3)
    return (
        jnp.where(low_one, b0, turn(b1, 1)),
        jnp.where(low_one, turn(b0, -1), b1),
        jnp.where(low_one, b2, turn(b3, 1)),
        jnp.where(low_one, turn(b2, -1), b3),
    )


def middle_sum(blocks):
    first, last = blocks[..., 0, :, :], blocks[..., 4, :, :]
    low = row_bit(first.shape, 1)
    new_last = last + jnp.where(low, turn(first, -1), 0.0)
    new_first = first + jnp.where(low, 0.0, turn(last, 1))
    return jnp.concatenate(
        [new_first[..., None, :, :], blocks[..., 1:4, :, :], new_last[..., None, :, :]], axis=-3
    )


def pack_half(blocks, low):
    half = (blocks.shape[0] + 1) // 2
    first, second = blocks[:half], blocks[half:]
    if second.shape[0] < half:
        second = jnp.concatenate([second, first[-1:]], axis=0)
    keep = row_bit(first.shape, 4)
    other = turn(second, 4)
    return jnp.where(keep, first, other) if low else jnp.where(keep, other, first)


def unpack_half(packed, count):
    return jnp.concatenate([packed, turn(packed, 4)], axis=0)[:count]


def kernel(
    regions,
    events,
    uf,
    vf,
    ua,
    va,
    source,
    lam,
    mu,
    rho,
    slope_two,
    slope_low,
    back_two,
    back_high,
    uf_out,
    vf_out,
    ua_out,
    va_out,
    k_out,
    u,
    b,
    sm,
    im,
    muw,
    lamw,
    gy,
    sx,
    sy,
    f,
    w8,
    kacc,
    send_a,
    recv_a,
    send_b,
    recv_b,
    send_l,
    recv_l,
    send_r,
    recv_r,
    send_8,
    recv_8,
    send_k,
    recv_k,
    sems,
    sems_8,
    sems_k,
):
    numbers, weights = gll_numbers()
    lanes = u.shape[-1]
    region, event = lax.axis_index("region"), lax.axis_index("event")
    left, right = lax.rem(region + regions - 1, regions), lax.rem(region + 1, regions)
    planes = 8 // events

    barrier = pltpu.get_barrier_semaphore()
    for other in range(events):
        for side in (left, right):
            pl.semaphore_signal(barrier, inc=1, device_id=(side, other), device_id_type=MESH)
    for offset in range(1, events):
        partner = lax.rem(event + offset, events)
        pl.semaphore_signal(barrier, inc=1, device_id=(region, partner), device_id_type=MESH)

    def remote(src, dst, number, target):
        return pltpu.make_async_remote_copy(
            src_ref=src,
            dst_ref=dst,
            send_sem=sems.at[0, number],
            recv_sem=sems.at[1, number],
            device_id=target,
            device_id_type=MESH,
        )

    one = (5, 8, lanes)
    low4, low2, low1 = row_bit(one, 4), row_bit(one, 2), row_bit(one, 1)
    lane_place = lax.broadcasted_iota(jnp.int32, one, 2) & 3
    lane_weight = jnp.where(
        lane_place == 0, 0.2, jnp.where(lane_place == 2, 32.0 / 45.0, 49.0 / 90.0)
    ).astype(jnp.float32)
    level = lax.broadcasted_iota(jnp.int32, one, 0)
    edge = (level == 0) | (level == 4)
    inner = jnp.where(level == 2, 32.0 / 45.0, 49.0 / 90.0)
    level_weight = jnp.where(edge, 0.1, inner).astype(jnp.float32)
    closed = ((level == 0) & low1) | ((level == 4) & jnp.logical_not(low1))
    node_weight = jnp.where(edge, jnp.where(closed, 0.1, 0.2), inner).astype(jnp.float32)

    def take(first, second):
        return swap_rows((first[0:5], first[4:9], second[0:5], second[4:9]))

    for comp in range(3):
        for place, value in enumerate(take(uf[comp], ua[comp])):
            u[place, comp] = value
    lam_here, mu_here = take(lam[...], lam[...]), take(mu[...], mu[...])
    edge_pair = jnp.where(low2, mu_here[0], lam_here[0])
    send_a[...] = pack_half(
        jnp.concatenate([u[0].reshape(15, 8, lanes), edge_pair], axis=0), True
    )
    pl.semaphore_wait(barrier, 2 * events + events - 1)
    copy_a = remote(send_a, recv_a, 0, (left, event))
    copy_a.start()

    rho_here = take(rho[...], rho[...])
    for place in range(4):
        weight = 0.2 if place == 0 else float(weights[place])
        im[place] = time_step / (rho_here[place] * (weight * (node_weight * lane_weight)))
    for comp in range(3):
        rates = take(vf[comp], va[comp])
        sources = take(jnp.zeros_like(source[comp]), source[comp])
        for place in range(4):
            pushed = sources[place] * im[place]
            sm[place, comp] = pushed
            b[place, comp] = rates[place] + pushed
    ahead = u[0] + time_step * b[0]
    send_b[...] = pack_half(
        jnp.concatenate([ahead.reshape(15, 8, lanes), time_step * im[0]], axis=0), True
    )
    copy_b = remote(send_b, recv_b, 1, (left, event))
    copy_b.start()

    for place in range(4):
        weight = float(weights[place]) * (level_weight * lane_weight)
        muw[place] = mu_here[place] * weight
        lamw[place] = lam_here[place] * weight

    def slopes(begin, end):
        rows = (end - begin) * 120
        values = u[begin:end].reshape(rows, lanes)
        high = values.astype(jnp.bfloat16)
        low = (values - high.astype(jnp.float32)).astype(jnp.bfloat16)
        found = jnp.dot(
            jnp.concatenate([high, low], axis=1), slope_two[...], preferred_element_type=jnp.float32
        ) + jnp.dot(high, slope_low[...], preferred_element_type=jnp.float32)
        gy[begin:end] = found.reshape(end - begin, 3, 5, 8, 2 * lanes)

    def strains(step):
        for i in range(5):
            gx = [combine(numbers[i], [u[q, c] for q in range(5)]) for c in range(3)]
            gz = []
            for c in range(3):
                levels = [u[i, c, q] for q in range(5)]
                gz.append(jnp.stack([combine(numbers[k], levels) for k in range(5)]))
            gm = [gy[i, c, :, :, :lanes] for c in range(3)]
            gd = [gy[i, c, :, :, lanes:] for c in range(3)]
            m, l = muw[i], lamw[i]
            xz, xy, zy = gx[1] + gz[0], gx[2] + gm[0], gz[2] + gm[1]
            dilation = gx[0] + gz[1] + gm[2]
            both = m + m
            press = l * dilation
            s_xz, s_xy, s_zy = m * xz, m * xy, m * zy
            sx[i, 0] = both * gx[0] + press
            sx[i, 1] = s_xz
            sx[i, 2] = s_xy
            sy[i, 0, :, :, :lanes] = s_xy
            sy[i, 1, :, :, :lanes] = s_zy
            sy[i, 2, :, :, :lanes] = both * gm[2] + press
            sy[i, 0, :, :, lanes:] = m * gd[0]
            sy[i, 1, :, :, lanes:] = m * gd[1]
            sy[i, 2, :, :, lanes:] = (both + l) * gd[2]
            for c, stress in enumerate((s_xz, both * gz[1] + press, s_zy)):
                levels = [stress[q] for q in range(5)]
                f[i, c] = jnp.stack([combine(numbers[:, k], levels) for k in range(5)])

            def product(value):
                return value * turn(value, -2)

            jump = product(gd[2])
            weight = float(weights[i]) * (level_weight * lane_weight)
            k1 = weight * (product(dilation) + jump)
            shear = product(gx[0]) + product(gz[1]) + product(gm[2]) + jump
            cross = product(xz) + product(xy) + product(zy) + product(gd[0]) + product(gd[1])
            k2 = weight * (2.0 * shear + cross)
            both_kinds = jnp.where(low2, k1, turn(k2, 2))
            kacc[i] = both_kinds if step == 0 else kacc[i] + both_kinds

    def gather_forces():
        rows = 600
        values = sy[...].reshape(rows, 2 * lanes)
        high = values.astype(jnp.bfloat16)
        low = (values - high.astype(jnp.float32)).astype(jnp.bfloat16)
        first = jnp.dot(high, back_two[...], preferred_element_type=jnp.float32)
        total = first[:, :lanes] + first[:, lanes:]
        total = total + jnp.dot(low, back_high[...], preferred_element_type=jnp.float32)
        total = total.reshape(5, 3, 5, 8, lanes)
        for i in (0, 4, 1, 2, 3):
            for c in range(3):
                value = f[i, c] + total[i, c] + combine(numbers[:, i], [sx[p, c] for p in range(5)])
                f[i, c] = middle_sum(value)

    slopes(0, 4)
    copy_a.wait_recv()
    arrived = unpack_half(recv_a[...], 20)
    wide = jnp.broadcast_to(row_bit((8, lanes), 4), (15, 8, lanes))
    next_plane = turn(jnp.where(wide, arrived[:15], u[0].reshape(15, 8, lanes)), 4)
    u[4] = next_plane.reshape(3, 5, 8, lanes)
    pair = arrived[15:]
    mu_next, lam_next = jnp.where(low2, pair, turn(pair, 2)), jnp.where(low2, turn(pair, -2), pair)
    weight = 0.1 * (level_weight * lane_weight)
    muw[4] = turn(jnp.where(low4, mu_next, mu_here[0]), 4) * weight
    lamw[4] = turn(jnp.where(low4, lam_next, lam_here[0]), 4) * weight
    slopes(4, 5)
    strains(0)
    gather_forces()
    send_l[...] = pack_half(f[0].reshape(15, 8, lanes), True)
    send_r[0] = pack_half(f[4].reshape(15, 8, lanes), False)
    copy_l = remote(send_l, recv_l, 2, (left, event))
    copy_l.start()
    copy_r = remote(send_r.at[0], recv_r.at[0], 3, (right, event))
    copy_r.start()

    def advance(place, force):
        for c in range(3):
            rate = b[place, c] - im[place] * force[c]
            b[place, c] = rate
            u[place, c] = u[place, c] + time_step * rate

    for place in (1, 2, 3):
        advance(place, f[place])
        b[place] = b[place] + sm[place]
    slopes(1, 4)
    copy_b.wait_recv()
    later = unpack_half(recv_b[...], 20)
    copy_l.wait_recv()
    from_right = unpack_half(recv_l[...], 15)
    own_last = f[4].reshape(15, 8, lanes)
    full = own_last + turn(from_right, 4)
    heavy = jnp.broadcast_to(later[15:][None], (3, 5, 8, lanes)).reshape(15, 8, lanes)
    u8 = turn(later[:15], 4) - turn(heavy, 4) * full

    def first_force(slot):
        from_left = unpack_half(recv_r[slot], 15)
        mixed = turn(jnp.where(wide, own_last_of(), from_left), 4)
        return (f[0].reshape(15, 8, lanes) + mixed).reshape(3, 5, 8, lanes)

    def own_last_of():
        return f[4].reshape(15, 8, lanes)

    copy_r.wait_recv()
    advance(0, first_force(0))
    b[0] = b[0] + sm[0]
    shared = turn(u[0].reshape(15, 8, lanes), 4)
    u[4] = jnp.where(wide, shared, u8).reshape(3, 5, 8, lanes)
    slopes(0, 1)
    slopes(4, 5)
    strains(1)
    gather_forces()
    send_r[1] = pack_half(f[4].reshape(15, 8, lanes), False)
    copy_s = remote(send_r.at[1], recv_r.at[1], 4, (right, event))
    copy_s.start()

    for i in range(5):
        kacc[i] = middle_sum(kacc[i])
    send_8[...] = kacc[4]
    copy_8 = pltpu.make_async_remote_copy(
        src_ref=send_8,
        dst_ref=recv_8.at[event],
        send_sem=sems.at[0, 5],
        recv_sem=sems_8.at[event],
        device_id=(right, 0),
        device_id_type=MESH,
    )
    copy_8.start()
    first_plane = kacc[0] + jnp.where(low4, 0.0, turn(kacc[4], 4))
    nodes = swap_rows((first_plane, kacc[1], kacc[2], kacc[3]))
    for kind in range(2):
        whole = jnp.concatenate([nodes[2 * kind][0:4], nodes[2 * kind + 1]], axis=0)
        for owner in range(events):
            send_k[owner, kind] = whole[:, planes * owner : planes * owner + planes]
    copies = []
    for offset in range(1, events):
        partner = lax.rem(event + offset, events)
        copy = pltpu.make_async_remote_copy(
            src_ref=send_k.at[partner],
            dst_ref=recv_k.at[offset - 1],
            send_sem=sems_k.at[0, offset - 1],
            recv_sem=sems_k.at[1, offset - 1],
            device_id=(region, partner),
            device_id_type=MESH,
        )
        copy.start()
        copies.append(copy)

    for place in (1, 2, 3):
        advance(place, f[place])
    copy_s.wait_recv()
    advance(0, first_force(1))

    def give(state, forward_out, adjoint_out):
        for c in range(3):
            four = swap_rows((state[0, c], state[1, c], state[2, c], state[3, c]))
            forward_out[c] = jnp.concatenate([four[0][0:4], four[1]], axis=0)
            adjoint_out[c] = jnp.concatenate([four[2][0:4], four[3]], axis=0)

    give(u, uf_out, ua_out)
    give(b, vf_out, va_out)

    total = send_k[event]
    for offset in range(1, events):
        copies[offset - 1].wait_recv()
        total = total + recv_k[offset - 1]
    k_out[...] = total

    @pl.when(event == 0)
    def _():
        extra = None
        for other in range(events):
            pltpu.make_async_copy(recv_8.at[other], recv_8.at[other], sems_8.at[other]).wait()
            extra = recv_8[other] if extra is None else extra + recv_8[other]
        extra = jnp.where(low4, turn(extra, 4), 0.0)
        nothing = jnp.zeros_like(extra)
        parts = swap_rows((extra, nothing, nothing, nothing))
        for kind in range(2):
            whole = jnp.concatenate([parts[2 * kind][0:4], parts[2 * kind + 1]], axis=0)
            k_out[kind] = k_out[kind] + whole[:, 0:planes]

    for copy in [copy_a, copy_b, copy_l, copy_r, copy_s, copy_8] + copies:
        copy.wait_send()


def run(regions, events, interpret, *arrays):
    lanes = arrays[0].shape[-1]
    fields = [jnp.transpose(array[0], (0, 2, 1, 3)) for array in arrays[:5]]
    models = [jnp.transpose(array, (1, 0, 2)) for array in arrays[5:]]
    tables = [jnp.asarray(table) for table in lane_tables(lanes)]
    planes = 8 // events
    state = jax.ShapeDtypeStruct((3, 9, 8, lanes), jnp.float32)
    f32 = jnp.float32
    vector = pltpu.VMEM((5, 3, 5, 8, lanes), f32)
    wide = pltpu.VMEM((5, 3, 5, 8, 2 * lanes), f32)
    scalar = pltpu.VMEM((5, 5, 8, lanes), f32)

    def packed(*lead):
        return pltpu.VMEM(lead + (8, lanes), f32)

    outs = pl.pallas_call(
        functools.partial(kernel, regions, events),
        out_shape=[state] * 4 + [jax.ShapeDtypeStruct((2, 9, planes, lanes), f32)],
        in_specs=[pl.BlockSpec(memory_space=pltpu.VMEM)] * 12,
        out_specs=[pl.BlockSpec(memory_space=pltpu.VMEM)] * 5,
        scratch_shapes=[
            vector,
            vector,
            vector,
            scalar,
            scalar,
            scalar,
            wide,
            vector,
            wide,
            vector,
            packed(15),
            scalar,
            packed(10),
            packed(10),
            packed(10),
            packed(10),
            packed(8),
            packed(8),
            packed(2, 8),
            packed(2, 8),
            packed(5),
            packed(events, 5),
            pltpu.VMEM((events, 2, 9, planes, lanes), f32),
            pltpu.VMEM((max(events - 1, 1), 2, 9, planes, lanes), f32),
            pltpu.SemaphoreType.DMA((2, 6)),
            pltpu.SemaphoreType.DMA((events,)),
            pltpu.SemaphoreType.DMA((2, max(events - 1, 1))),
        ],
        compiler_params=pltpu.CompilerParams(
            collective_id=0, has_side_effects=True, vmem_limit_bytes=40 * 1024 * 1024
        ),
        name="adjoint_steps",
    )(*fields, *models, *tables)
    forward, forward_rate, adjoint, adjoint_rate = [
        jnp.transpose(out, (0, 2, 1, 3))[None] for out in outs[:4]
    ]
    return (forward, forward_rate, adjoint, adjoint_rate, jnp.transpose(outs[4], (0, 2, 1, 3)))


def solution(mesh):
    field = P("event", None, "region", None, None)
    model = P("region", None, None)
    regions, events = mesh.shape["region"], mesh.shape["event"]
    return jax.shard_map(
        functools.partial(run, regions, events, False),
        mesh=mesh,
        in_specs=(field,) * 5 + (model,) * 3,
        out_specs=(field,) * 4 + (P(None, ("region", "event"), None, None),),
        check_vma=False,
    )
```

```python
import functools
import math

import jax
import jax.numpy as jnp
import numpy as np
from jax import lax
from jax.experimental import pallas as pl
from jax.experimental.pallas import tpu as pltpu
from jax.sharding import PartitionSpec as P

STEPS = 2
time_step = 0.02
MESH = pl.DeviceIdType.MESH


def gll_numbers():
    points = np.array([-1.0, -math.sqrt(3.0 / 7.0), 0.0, math.sqrt(3.0 / 7.0), 1.0])
    weights = np.array([0.1, 49.0 / 90.0, 32.0 / 45.0, 49.0 / 90.0, 0.1])
    legendre = (35.0 * points**4 - 30.0 * points**2 + 3.0) / 8.0
    derivative = np.zeros((5, 5))
    for target in range(5):
        for column in range(5):
            if target != column:
                derivative[target, column] = legendre[target] / (
                    legendre[column] * (points[target] - points[column])
                )
    derivative[0, 0] = -5.0
    derivative[4, 4] = 5.0
    return (derivative, weights)


def lane_tables(lanes):
    numbers, _ = gll_numbers()
    table = np.zeros((lanes, 2 * lanes))
    for lane in range(lanes):
        start, local = lane - lane % 4, lane % 4
        for source in range(5):
            if local:
                table[(start + source) % lanes, lane] += numbers[local, source]
            else:
                right, left = (start + source) % lanes, (start - 4 + source) % lanes
                table[right, lane] += 0.5 * numbers[0, source]
                table[left, lane] += 0.5 * numbers[4, source]
                table[right, lanes + lane] += 0.5 * numbers[0, source]
                table[left, lanes + lane] -= 0.5 * numbers[4, source]
    high = table.astype(np.float32).astype(jnp.bfloat16)
    low = (table - high.astype(np.float64)).astype(np.float32).astype(jnp.bfloat16)
    return (
        np.concatenate([high, high], axis=0),
        low,
        np.concatenate([high.T, low.T], axis=1),
        np.ascontiguousarray(high.T),
    )


def combine(coefficients, pieces):
    total = None
    for number, piece in zip(coefficients, pieces):
        if number != 0.0:
            term = float(number) * piece
            total = term if total is None else total + term
    return total


def turn(value, shift):
    return pltpu.roll(value, shift % 8, value.ndim - 2)


def row_bit(shape, bit):
    return (lax.broadcasted_iota(jnp.int32, shape, len(shape) - 2) & bit) == 0


def swap_rows(four):
    shape = four[0].shape
    low_two, low_one = row_bit(shape, 2), row_bit(shape, 1)
    a0, a1, a2, a3 = four
    b0 = jnp.where(low_two, a0, turn(a2, 2))
    b2 = jnp.where(low_two, turn(a0, -2), a2)
    b1 = jnp.where(low_two, a1, turn(a3, 2))
    b3 = jnp.where(low_two, turn(a1, -2), a3)
    return (
        jnp.where(low_one, b0, turn(b1, 1)),
        jnp.where(low_one, turn(b0, -1), b1),
        jnp.where(low_one, b2, turn(b3, 1)),
        jnp.where(low_one, turn(b2, -1), b3),
    )


def middle_sum(blocks):
    first, last = blocks[..., 0, :, :], blocks[..., 4, :, :]
    low = row_bit(first.shape, 1)
    new_last = last + jnp.where(low, turn(first, -1), 0.0)
    new_first = first + jnp.where(low, 0.0, turn(last, 1))
    return jnp.concatenate(
        [new_first[..., None, :, :], blocks[..., 1:4, :, :], new_last[..., None, :, :]], axis=-3
    )


def pack_half(blocks, low):
    half = (blocks.shape[0] + 1) // 2
    first, second = blocks[:half], blocks[half:]
    if second.shape[0] < half:
        second = jnp.concatenate([second, first[-1:]], axis=0)
    keep = row_bit(first.shape, 4)
    other = turn(second, 4)
    return jnp.where(keep, first, other) if low else jnp.where(keep, other, first)


def unpack_half(packed, count):
    return jnp.concatenate([packed, turn(packed, 4)], axis=0)[:count]


def kernel(
    regions,
    events,
    uf_in,
    vf_in,
    ua_in,
    va_in,
    source_in,
    lam_in,
    mu_in,
    rho_in,
    slope_two_in,
    slope_low_in,
    back_two_in,
    back_high_in,
    uf_out,
    vf_out,
    ua_out,
    va_out,
    k_out,
    u,
    b,
    sm,
    im,
    muw,
    lamw,
    gy,
    sx,
    sy,
    f,
    w8,
    kacc,
    send_a,
    recv_a,
    send_b,
    recv_b,
    send_l,
    recv_l,
    send_r,
    recv_r,
    send_8,
    recv_8,
    send_k,
    recv_k,
    sems,
    sems_8,
    sems_k,
    uf,
    vf,
    ua,
    va,
    source,
    lam,
    mu,
    rho,
    slope_two,
    slope_low,
    back_two,
    back_high,
    load_sems,
):
    numbers, weights = gll_numbers()
    lanes = u.shape[-1]
    region, event = lax.axis_index("region"), lax.axis_index("event")
    left, right = lax.rem(region + regions - 1, regions), lax.rem(region + 1, regions)
    planes = 8 // events

    barrier = pltpu.get_barrier_semaphore()
    for other in range(events):
        for side in (left, right):
            pl.semaphore_signal(barrier, inc=1, device_id=(side, other), device_id_type=MESH)
    for offset in range(1, events):
        partner = lax.rem(event + offset, events)
        pl.semaphore_signal(barrier, inc=1, device_id=(region, partner), device_id_type=MESH)

    loads = {}
    for number, (name, src, dst) in enumerate(
        (
            ("uf", uf_in, uf),
            ("ua", ua_in, ua),
            ("lam", lam_in, lam),
            ("mu", mu_in, mu),
            ("rho", rho_in, rho),
            ("vf", vf_in, vf),
            ("va", va_in, va),
            ("source", source_in, source),
            ("slope_two", slope_two_in, slope_two),
            ("slope_low", slope_low_in, slope_low),
            ("back_two", back_two_in, back_two),
            ("back_high", back_high_in, back_high),
        )
    ):
        loads[name] = pltpu.make_async_copy(src, dst, load_sems.at[number])
        loads[name].start()

    def ready(*names):
        for name in names:
            loads[name].wait()

    def remote(src, dst, number, target):
        return pltpu.make_async_remote_copy(
            src_ref=src,
            dst_ref=dst,
            send_sem=sems.at[0, number],
            recv_sem=sems.at[1, number],
            device_id=target,
            device_id_type=MESH,
        )

    one = (5, 8, lanes)
    low4, low2, low1 = row_bit(one, 4), row_bit(one, 2), row_bit(one, 1)
    lane_place = lax.broadcasted_iota(jnp.int32, one, 2) & 3
    lane_weight = jnp.where(
        lane_place == 0, 0.2, jnp.where(lane_place == 2, 32.0 / 45.0, 49.0 / 90.0)
    ).astype(jnp.float32)
    level = lax.broadcasted_iota(jnp.int32, one, 0)
    edge = (level == 0) | (level == 4)
    inner = jnp.where(level == 2, 32.0 / 45.0, 49.0 / 90.0)
    level_weight = jnp.where(edge, 0.1, inner).astype(jnp.float32)
    closed = ((level == 0) & low1) | ((level == 4) & jnp.logical_not(low1))
    node_weight = jnp.where(edge, jnp.where(closed, 0.1, 0.2), inner).astype(jnp.float32)

    def take(first, second):
        return swap_rows((first[0:5], first[4:9], second[0:5], second[4:9]))

    ready("uf", "ua")
    for comp in range(3):
        for place, value in enumerate(take(uf[comp], ua[comp])):
            u[place, comp] = value
    ready("lam", "mu")
    lam_here, mu_here = take(lam[...], lam[...]), take(mu[...], mu[...])
    edge_pair = jnp.where(low2, mu_here[0], lam_here[0])
    send_a[...] = pack_half(
        jnp.concatenate([u[0].reshape(15, 8, lanes), edge_pair], axis=0), True
    )
    pl.semaphore_wait(barrier, 2 * events + events - 1)
    copy_a = remote(send_a, recv_a, 0, (left, event))
    copy_a.start()

    ready("rho")
    rho_here = take(rho[...], rho[...])
    for place in range(4):
        weight = 0.2 if place == 0 else float(weights[place])
        im[place] = time_step / (rho_here[place] * (weight * (node_weight * lane_weight)))
    ready("vf", "va", "source")
    for comp in range(3):
        rates = take(vf[comp], va[comp])
        sources = take(jnp.zeros_like(source[comp]), source[comp])
        for place in range(4):
            pushed = sources[place] * im[place]
            sm[place, comp] = pushed
            b[place, comp] = rates[place] + pushed
    ahead = u[0] + time_step * b[0]
    send_b[...] = pack_half(
        jnp.concatenate([ahead.reshape(15, 8, lanes), time_step * im[0]], axis=0), True
    )
    copy_b = remote(send_b, recv_b, 1, (left, event))
    copy_b.start()

    for place in range(4):
        weight = float(weights[place]) * (level_weight * lane_weight)
        muw[place] = mu_here[place] * weight
        lamw[place] = lam_here[place] * weight

    def slopes(begin, end):
        rows = (end - begin) * 120
        values = u[begin:end].reshape(rows, lanes)
        high = values.astype(jnp.bfloat16)
        low = (values - high.astype(jnp.float32)).astype(jnp.bfloat16)
        found = jnp.dot(
            jnp.concatenate([high, low], axis=1), slope_two[...], preferred_element_type=jnp.float32
        ) + jnp.dot(high, slope_low[...], preferred_element_type=jnp.float32)
        gy[begin:end] = found.reshape(end - begin, 3, 5, 8, 2 * lanes)

    def strains(step):
        for i in range(5):
            gx = [combine(numbers[i], [u[q, c] for q in range(5)]) for c in range(3)]
            gz = []
            for c in range(3):
                levels = [u[i, c, q] for q in range(5)]
                gz.append(jnp.stack([combine(numbers[k], levels) for k in range(5)]))
            gm = [gy[i, c, :, :, :lanes] for c in range(3)]
            gd = [gy[i, c, :, :, lanes:] for c in range(3)]
            m, l = muw[i], lamw[i]
            xz, xy, zy = gx[1] + gz[0], gx[2] + gm[0], gz[2] + gm[1]
            dilation = gx[0] + gz[1] + gm[2]
            both = m + m
            press = l * dilation
            s_xz, s_xy, s_zy = m * xz, m * xy, m * zy
            sx[i, 0] = both * gx[0] + press
            sx[i, 1] = s_xz
            sx[i, 2] = s_xy
            sy[i, 0, :, :, :lanes] = s_xy
            sy[i, 1, :, :, :lanes] = s_zy
            sy[i, 2, :, :, :lanes] = both * gm[2] + press
            sy[i, 0, :, :, lanes:] = m * gd[0]
            sy[i, 1, :, :, lanes:] = m * gd[1]
            sy[i, 2, :, :, lanes:] = (both + l) * gd[2]
            for c, stress in enumerate((s_xz, both * gz[1] + press, s_zy)):
                levels = [stress[q] for q in range(5)]
                f[i, c] = jnp.stack([combine(numbers[:, k], levels) for k in range(5)])

            def product(value):
                return value * turn(value, -2)

            jump = product(gd[2])
            weight = float(weights[i]) * (level_weight * lane_weight)
            k1 = weight * (product(dilation) + jump)
            shear = product(gx[0]) + product(gz[1]) + product(gm[2]) + jump
            cross = product(xz) + product(xy) + product(zy) + product(gd[0]) + product(gd[1])
            k2 = weight * (2.0 * shear + cross)
            both_kinds = jnp.where(low2, k1, turn(k2, 2))
            kacc[i] = both_kinds if step == 0 else kacc[i] + both_kinds

    def gather_forces():
        rows = 600
        values = sy[...].reshape(rows, 2 * lanes)
        high = values.astype(jnp.bfloat16)
        low = (values - high.astype(jnp.float32)).astype(jnp.bfloat16)
        first = jnp.dot(high, back_two[...], preferred_element_type=jnp.float32)
        total = first[:, :lanes] + first[:, lanes:]
        total = total + jnp.dot(low, back_high[...], preferred_element_type=jnp.float32)
        total = total.reshape(5, 3, 5, 8, lanes)
        for i in (0, 4, 1, 2, 3):
            for c in range(3):
                value = f[i, c] + total[i, c] + combine(numbers[:, i], [sx[p, c] for p in range(5)])
                f[i, c] = middle_sum(value)

    ready("slope_two", "slope_low", "back_two", "back_high")
    slopes(0, 4)
    copy_a.wait_recv()
    arrived = unpack_half(recv_a[...], 20)
    wide = jnp.broadcast_to(row_bit((8, lanes), 4), (15, 8, lanes))
    next_plane = turn(jnp.where(wide, arrived[:15], u[0].reshape(15, 8, lanes)), 4)
    u[4] = next_plane.reshape(3, 5, 8, lanes)
    pair = arrived[15:]
    mu_next, lam_next = jnp.where(low2, pair, turn(pair, 2)), jnp.where(low2, turn(pair, -2), pair)
    weight = 0.1 * (level_weight * lane_weight)
    muw[4] = turn(jnp.where(low4, mu_next, mu_here[0]), 4) * weight
    lamw[4] = turn(jnp.where(low4, lam_next, lam_here[0]), 4) * weight
    slopes(4, 5)
    strains(0)
    gather_forces()
    send_l[...] = pack_half(f[0].reshape(15, 8, lanes), True)
    send_r[0] = pack_half(f[4].reshape(15, 8, lanes), False)
    copy_l = remote(send_l, recv_l, 2, (left, event))
    copy_l.start()
    copy_r = remote(send_r.at[0], recv_r.at[0], 3, (right, event))
    copy_r.start()

    def advance(place, force):
        for c in range(3):
            rate = b[place, c] - im[place] * force[c]
            b[place, c] = rate
            u[place, c] = u[place, c] + time_step * rate

    for place in (1, 2, 3):
        advance(place, f[place])
        b[place] = b[place] + sm[place]
    slopes(1, 4)
    copy_b.wait_recv()
    later = unpack_half(recv_b[...], 20)
    copy_l.wait_recv()
    from_right = unpack_half(recv_l[...], 15)
    own_last = f[4].reshape(15, 8, lanes)
    full = own_last + turn(from_right, 4)
    heavy = jnp.broadcast_to(later[15:][None], (3, 5, 8, lanes)).reshape(15, 8, lanes)
    u8 = turn(later[:15], 4) - turn(heavy, 4) * full

    def first_force(slot):
        from_left = unpack_half(recv_r[slot], 15)
        mixed = turn(jnp.where(wide, own_last_of(), from_left), 4)
        return (f[0].reshape(15, 8, lanes) + mixed).reshape(3, 5, 8, lanes)

    def own_last_of():
        return f[4].reshape(15, 8, lanes)

    copy_r.wait_recv()
    advance(0, first_force(0))
    b[0] = b[0] + sm[0]
    shared = turn(u[0].reshape(15, 8, lanes), 4)
    u[4] = jnp.where(wide, shared, u8).reshape(3, 5, 8, lanes)
    slopes(0, 1)
    slopes(4, 5)
    strains(1)
    gather_forces()
    send_r[1] = pack_half(f[4].reshape(15, 8, lanes), False)
    copy_s = remote(send_r.at[1], recv_r.at[1], 4, (right, event))
    copy_s.start()

    for i in range(5):
        kacc[i] = middle_sum(kacc[i])
    send_8[...] = kacc[4]
    copy_8 = pltpu.make_async_remote_copy(
        src_ref=send_8,
        dst_ref=recv_8.at[event],
        send_sem=sems.at[0, 5],
        recv_sem=sems_8.at[event],
        device_id=(right, 0),
        device_id_type=MESH,
    )
    copy_8.start()
    first_plane = kacc[0] + jnp.where(low4, 0.0, turn(kacc[4], 4))
    nodes = swap_rows((first_plane, kacc[1], kacc[2], kacc[3]))
    for kind in range(2):
        whole = jnp.concatenate([nodes[2 * kind][0:4], nodes[2 * kind + 1]], axis=0)
        for owner in range(events):
            send_k[owner, kind] = whole[:, planes * owner : planes * owner + planes]
    copies = []
    for offset in range(1, events):
        partner = lax.rem(event + offset, events)
        copy = pltpu.make_async_remote_copy(
            src_ref=send_k.at[partner],
            dst_ref=recv_k.at[offset - 1],
            send_sem=sems_k.at[0, offset - 1],
            recv_sem=sems_k.at[1, offset - 1],
            device_id=(region, partner),
            device_id_type=MESH,
        )
        copy.start()
        copies.append(copy)

    for place in (1, 2, 3):
        advance(place, f[place])
    copy_s.wait_recv()
    advance(0, first_force(1))

    def give(state, forward_out, adjoint_out):
        for c in range(3):
            four = swap_rows((state[0, c], state[1, c], state[2, c], state[3, c]))
            forward_out[c] = jnp.concatenate([four[0][0:4], four[1]], axis=0)
            adjoint_out[c] = jnp.concatenate([four[2][0:4], four[3]], axis=0)

    give(u, uf_out, ua_out)
    give(b, vf_out, va_out)

    total = send_k[event]
    for offset in range(1, events):
        copies[offset - 1].wait_recv()
        total = total + recv_k[offset - 1]
    k_out[...] = total

    @pl.when(event == 0)
    def _():
        extra = None
        for other in range(events):
            pltpu.make_async_copy(recv_8.at[other], recv_8.at[other], sems_8.at[other]).wait()
            extra = recv_8[other] if extra is None else extra + recv_8[other]
        extra = jnp.where(low4, turn(extra, 4), 0.0)
        nothing = jnp.zeros_like(extra)
        parts = swap_rows((extra, nothing, nothing, nothing))
        for kind in range(2):
            whole = jnp.concatenate([parts[2 * kind][0:4], parts[2 * kind + 1]], axis=0)
            k_out[kind] = k_out[kind] + whole[:, 0:planes]

    for copy in [copy_a, copy_b, copy_l, copy_r, copy_s, copy_8] + copies:
        copy.wait_send()


def flush(*refs):
    copies = [pltpu.make_async_copy(refs[n], refs[5 + n], refs[10].at[n]) for n in range(5)]
    for copy in copies:
        copy.start()
    for copy in copies:
        copy.wait()


def run(regions, events, interpret, *arrays):
    lanes = arrays[0].shape[-1]
    fields = [jnp.transpose(array[0], (0, 2, 1, 3)) for array in arrays[:5]]
    models = [jnp.transpose(array, (1, 0, 2)) for array in arrays[5:]]
    tables = [jnp.asarray(table) for table in lane_tables(lanes)]
    operands = [*fields, *models, *tables]
    planes = 8 // events
    state = jax.ShapeDtypeStruct((3, 9, 8, lanes), jnp.float32)
    f32 = jnp.float32
    vector = pltpu.VMEM((5, 3, 5, 8, lanes), f32)
    wide = pltpu.VMEM((5, 3, 5, 8, 2 * lanes), f32)
    scalar = pltpu.VMEM((5, 5, 8, lanes), f32)

    def packed(*lead):
        return pltpu.VMEM(lead + (8, lanes), f32)

    outs = pl.pallas_call(
        functools.partial(kernel, regions, events),
        out_shape=[state] * 4 + [jax.ShapeDtypeStruct((2, 9, planes, lanes), f32)],
        in_specs=[pl.BlockSpec(memory_space=pltpu.HBM)] * 12,
        out_specs=[pl.BlockSpec(memory_space=pltpu.VMEM)] * 5,
        scratch_shapes=[
            vector,
            vector,
            vector,
            scalar,
            scalar,
            scalar,
            wide,
            vector,
            wide,
            vector,
            packed(15),
            scalar,
            packed(10),
            packed(10),
            packed(10),
            packed(10),
            packed(8),
            packed(8),
            packed(2, 8),
            packed(2, 8),
            packed(5),
            packed(events, 5),
            pltpu.VMEM((events, 2, 9, planes, lanes), f32),
            pltpu.VMEM((max(events - 1, 1), 2, 9, planes, lanes), f32),
            pltpu.SemaphoreType.DMA((2, 6)),
            pltpu.SemaphoreType.DMA((events,)),
            pltpu.SemaphoreType.DMA((2, max(events - 1, 1))),
            *[pltpu.VMEM(array.shape, array.dtype) for array in operands],
            pltpu.SemaphoreType.DMA((len(operands),)),
        ],
        compiler_params=pltpu.CompilerParams(
            collective_id=0, has_side_effects=True, vmem_limit_bytes=63 * 1024 * 1024
        ),
        name="adjoint_steps",
    )(*operands)
    outs = pl.pallas_call(
        flush,
        out_shape=[jax.ShapeDtypeStruct(out.shape, out.dtype) for out in outs],
        in_specs=[pl.BlockSpec(memory_space=pl.ANY)] * 5,
        out_specs=[pl.BlockSpec(memory_space=pltpu.HBM)] * 5,
        scratch_shapes=[pltpu.SemaphoreType.DMA((5,))],
        name="write_out",
    )(*outs)
    forward, forward_rate, adjoint, adjoint_rate = [
        jnp.transpose(out, (0, 2, 1, 3))[None] for out in outs[:4]
    ]
    return (forward, forward_rate, adjoint, adjoint_rate, jnp.transpose(outs[4], (0, 2, 1, 3)))


def solution(mesh):
    field = P("event", None, "region", None, None)
    model = P("region", None, None)
    regions, events = mesh.shape["region"], mesh.shape["event"]
    return jax.shard_map(
        functools.partial(run, regions, events, False),
        mesh=mesh,
        in_specs=(field,) * 5 + (model,) * 3,
        out_specs=(field,) * 4 + (P(None, ("region", "event"), None, None),),
        check_vma=False,
    )
```

```python
import functools
import math

import jax
import jax.numpy as jnp
import numpy as np
from jax import lax
from jax.experimental import pallas as pl
from jax.experimental.pallas import tpu as pltpu
from jax.sharding import PartitionSpec as P

STEPS = 2
time_step = 0.02
MESH = pl.DeviceIdType.MESH


def gll_numbers():
    points = np.array([-1.0, -math.sqrt(3.0 / 7.0), 0.0, math.sqrt(3.0 / 7.0), 1.0])
    weights = np.array([0.1, 49.0 / 90.0, 32.0 / 45.0, 49.0 / 90.0, 0.1])
    legendre = (35.0 * points**4 - 30.0 * points**2 + 3.0) / 8.0
    derivative = np.zeros((5, 5))
    for target in range(5):
        for column in range(5):
            if target != column:
                derivative[target, column] = legendre[target] / (
                    legendre[column] * (points[target] - points[column])
                )
    derivative[0, 0] = -5.0
    derivative[4, 4] = 5.0
    return (derivative, weights)


def lane_tables(lanes):
    numbers, _ = gll_numbers()
    table = np.zeros((lanes, 2 * lanes))
    for lane in range(lanes):
        start, local = lane - lane % 4, lane % 4
        for source in range(5):
            if local:
                table[(start + source) % lanes, lane] += numbers[local, source]
            else:
                right, left = (start + source) % lanes, (start - 4 + source) % lanes
                table[right, lane] += 0.5 * numbers[0, source]
                table[left, lane] += 0.5 * numbers[4, source]
                table[right, lanes + lane] += 0.5 * numbers[0, source]
                table[left, lanes + lane] -= 0.5 * numbers[4, source]
    high = table.astype(np.float32).astype(jnp.bfloat16)
    low = (table - high.astype(np.float64)).astype(np.float32).astype(jnp.bfloat16)
    return (
        np.concatenate([high, high], axis=0),
        low,
        np.concatenate([high.T, low.T], axis=1),
        np.ascontiguousarray(high.T),
    )


def combine(coefficients, pieces):
    total = None
    for number, piece in zip(coefficients, pieces):
        if number != 0.0:
            term = float(number) * piece
            total = term if total is None else total + term
    return total


def turn(value, shift):
    return pltpu.roll(value, shift % 8, value.ndim - 2)


def row_bit(shape, bit):
    return (lax.broadcasted_iota(jnp.int32, shape, len(shape) - 2) & bit) == 0


def swap_rows(four):
    shape = four[0].shape
    low_two, low_one = row_bit(shape, 2), row_bit(shape, 1)
    a0, a1, a2, a3 = four
    b0 = jnp.where(low_two, a0, turn(a2, 2))
    b2 = jnp.where(low_two, turn(a0, -2), a2)
    b1 = jnp.where(low_two, a1, turn(a3, 2))
    b3 = jnp.where(low_two, turn(a1, -2), a3)
    return (
        jnp.where(low_one, b0, turn(b1, 1)),
        jnp.where(low_one, turn(b0, -1), b1),
        jnp.where(low_one, b2, turn(b3, 1)),
        jnp.where(low_one, turn(b2, -1), b3),
    )


def middle_sum(blocks):
    first, last = blocks[..., 0, :, :], blocks[..., 4, :, :]
    low = row_bit(first.shape, 1)
    new_last = last + jnp.where(low, turn(first, -1), 0.0)
    new_first = first + jnp.where(low, 0.0, turn(last, 1))
    return jnp.concatenate(
        [new_first[..., None, :, :], blocks[..., 1:4, :, :], new_last[..., None, :, :]], axis=-3
    )


def pack_half(blocks, low):
    half = (blocks.shape[0] + 1) // 2
    first, second = blocks[:half], blocks[half:]
    if second.shape[0] < half:
        second = jnp.concatenate([second, first[-1:]], axis=0)
    keep = row_bit(first.shape, 4)
    other = turn(second, 4)
    return jnp.where(keep, first, other) if low else jnp.where(keep, other, first)


def unpack_half(packed, count):
    return jnp.concatenate([packed, turn(packed, 4)], axis=0)[:count]


def kernel(
    regions,
    events,
    uf_in,
    vf_in,
    ua_in,
    va_in,
    source_in,
    lam_in,
    mu_in,
    rho_in,
    slope_two_in,
    slope_low_in,
    back_two_in,
    back_high_in,
    uf_out,
    vf_out,
    ua_out,
    va_out,
    k_out,
    u,
    b,
    sm,
    im,
    muw,
    lamw,
    gy,
    sx,
    sy,
    f,
    w8,
    kacc,
    send_a,
    recv_a,
    send_b,
    recv_b,
    send_l,
    recv_l,
    send_r,
    recv_r,
    send_8,
    recv_8,
    send_k,
    recv_k,
    sems,
    sems_8,
    sems_k,
    uf,
    vf,
    ua,
    va,
    source,
    lam,
    mu,
    rho,
    slope_two,
    slope_low,
    back_two,
    back_high,
    load_sems,
):
    numbers, weights = gll_numbers()
    lanes = u.shape[-1]
    region, event = lax.axis_index("region"), lax.axis_index("event")
    left, right = lax.rem(region + regions - 1, regions), lax.rem(region + 1, regions)
    planes = 8 // events

    barrier = pltpu.get_barrier_semaphore()
    for other in range(events):
        for side in (left, right):
            pl.semaphore_signal(barrier, inc=1, device_id=(side, other), device_id_type=MESH)
    for offset in range(1, events):
        partner = lax.rem(event + offset, events)
        pl.semaphore_signal(barrier, inc=1, device_id=(region, partner), device_id_type=MESH)

    loads = {}
    for number, (name, src, dst) in enumerate(
        (
            ("uf", uf_in, uf),
            ("ua", ua_in, ua),
            ("lam", lam_in, lam),
            ("mu", mu_in, mu),
            ("rho", rho_in, rho),
            ("vf", vf_in, vf),
            ("va", va_in, va),
            ("source", source_in, source),
            ("slope_two", slope_two_in, slope_two),
            ("slope_low", slope_low_in, slope_low),
            ("back_two", back_two_in, back_two),
            ("back_high", back_high_in, back_high),
        )
    ):
        loads[name] = pltpu.make_async_copy(src, dst, load_sems.at[number])
        loads[name].start()

    def ready(*names):
        for name in names:
            loads[name].wait()

    def remote(src, dst, number, target):
        return pltpu.make_async_remote_copy(
            src_ref=src,
            dst_ref=dst,
            send_sem=sems.at[0, number],
            recv_sem=sems.at[1, number],
            device_id=target,
            device_id_type=MESH,
        )

    one = (5, 8, lanes)
    low4, low2, low1 = row_bit(one, 4), row_bit(one, 2), row_bit(one, 1)
    lane_place = lax.broadcasted_iota(jnp.int32, one, 2) & 3
    lane_weight = jnp.where(
        lane_place == 0, 0.2, jnp.where(lane_place == 2, 32.0 / 45.0, 49.0 / 90.0)
    ).astype(jnp.float32)
    level = lax.broadcasted_iota(jnp.int32, one, 0)
    edge = (level == 0) | (level == 4)
    inner = jnp.where(level == 2, 32.0 / 45.0, 49.0 / 90.0)
    level_weight = jnp.where(edge, 0.1, inner).astype(jnp.float32)
    closed = ((level == 0) & low1) | ((level == 4) & jnp.logical_not(low1))
    node_weight = jnp.where(edge, jnp.where(closed, 0.1, 0.2), inner).astype(jnp.float32)

    def take(first, second):
        return swap_rows((first[0:5], first[4:9], second[0:5], second[4:9]))

    ready("uf", "ua")
    for comp in range(3):
        for place, value in enumerate(take(uf[comp], ua[comp])):
            u[place, comp] = value
    ready("lam", "mu")
    lam_here, mu_here = take(lam[...], lam[...]), take(mu[...], mu[...])
    edge_pair = jnp.where(low2, mu_here[0], lam_here[0])
    send_a[...] = pack_half(
        jnp.concatenate([u[0].reshape(15, 8, lanes), edge_pair], axis=0), True
    )
    pl.semaphore_wait(barrier, 2 * events + events - 1)
    copy_a = remote(send_a, recv_a, 0, (left, event))
    copy_a.start()

    ready("rho")
    rho_here = take(rho[...], rho[...])
    for place in range(4):
        weight = 0.2 if place == 0 else float(weights[place])
        im[place] = time_step / (rho_here[place] * (weight * (node_weight * lane_weight)))
    ready("vf", "va", "source")
    for comp in range(3):
        rates = take(vf[comp], va[comp])
        sources = take(jnp.zeros_like(source[comp]), source[comp])
        for place in range(4):
            pushed = sources[place] * im[place]
            sm[place, comp] = pushed
            b[place, comp] = rates[place] + pushed
    ahead = u[0] + time_step * b[0]
    send_b[...] = pack_half(
        jnp.concatenate([ahead.reshape(15, 8, lanes), time_step * im[0]], axis=0), True
    )
    copy_b = remote(send_b, recv_b, 1, (left, event))
    copy_b.start()

    for place in range(4):
        weight = float(weights[place]) * (level_weight * lane_weight)
        muw[place] = mu_here[place] * weight
        lamw[place] = lam_here[place] * weight

    def slopes(begin, end):
        rows = (end - begin) * 120
        values = u[begin:end].reshape(rows, lanes)
        high = values.astype(jnp.bfloat16)
        low = (values - high.astype(jnp.float32)).astype(jnp.bfloat16)
        found = jnp.dot(
            jnp.concatenate([high, low], axis=1), slope_two[...], preferred_element_type=jnp.float32
        ) + jnp.dot(high, slope_low[...], preferred_element_type=jnp.float32)
        gy[begin:end] = found.reshape(end - begin, 3, 5, 8, 2 * lanes)

    def strains(step):
        for i in range(5):
            gx = [combine(numbers[i], [u[q, c] for q in range(5)]) for c in range(3)]
            gz = []
            for c in range(3):
                levels = [u[i, c, q] for q in range(5)]
                gz.append(jnp.stack([combine(numbers[k], levels) for k in range(5)]))
            gm = [gy[i, c, :, :, :lanes] for c in range(3)]
            gd = [gy[i, c, :, :, lanes:] for c in range(3)]
            m, l = muw[i], lamw[i]
            xz, xy, zy = gx[1] + gz[0], gx[2] + gm[0], gz[2] + gm[1]
            dilation = gx[0] + gz[1] + gm[2]
            both = m + m
            press = l * dilation
            s_xz, s_xy, s_zy = m * xz, m * xy, m * zy
            sx[i, 0] = both * gx[0] + press
            sx[i, 1] = s_xz
            sx[i, 2] = s_xy
            sy[i, 0, :, :, :lanes] = s_xy
            sy[i, 1, :, :, :lanes] = s_zy
            sy[i, 2, :, :, :lanes] = both * gm[2] + press
            sy[i, 0, :, :, lanes:] = m * gd[0]
            sy[i, 1, :, :, lanes:] = m * gd[1]
            sy[i, 2, :, :, lanes:] = (both + l) * gd[2]
            for c, stress in enumerate((s_xz, both * gz[1] + press, s_zy)):
                levels = [stress[q] for q in range(5)]
                f[i, c] = jnp.stack([combine(numbers[:, k], levels) for k in range(5)])

            def product(value):
                return value * turn(value, -2)

            jump = product(gd[2])
            weight = float(weights[i]) * (level_weight * lane_weight)
            k1 = weight * (product(dilation) + jump)
            shear = product(gx[0]) + product(gz[1]) + product(gm[2]) + jump
            cross = product(xz) + product(xy) + product(zy) + product(gd[0]) + product(gd[1])
            k2 = weight * (2.0 * shear + cross)
            both_kinds = jnp.where(low2, k1, turn(k2, 2))
            kacc[i] = both_kinds if step == 0 else kacc[i] + both_kinds

    def gather_forces():
        rows = 600
        values = sy[...].reshape(rows, 2 * lanes)
        high = values.astype(jnp.bfloat16)
        low = (values - high.astype(jnp.float32)).astype(jnp.bfloat16)
        first = jnp.dot(high, back_two[...], preferred_element_type=jnp.float32)
        total = first[:, :lanes] + first[:, lanes:]
        total = total + jnp.dot(low, back_high[...], preferred_element_type=jnp.float32)
        total = total.reshape(5, 3, 5, 8, lanes)
        for i in (0, 4, 1, 2, 3):
            for c in range(3):
                value = f[i, c] + total[i, c] + combine(numbers[:, i], [sx[p, c] for p in range(5)])
                f[i, c] = middle_sum(value)

    ready("slope_two", "slope_low", "back_two", "back_high")
    slopes(0, 4)
    copy_a.wait_recv()
    arrived = unpack_half(recv_a[...], 20)
    wide = jnp.broadcast_to(row_bit((8, lanes), 4), (15, 8, lanes))
    next_plane = turn(jnp.where(wide, arrived[:15], u[0].reshape(15, 8, lanes)), 4)
    u[4] = next_plane.reshape(3, 5, 8, lanes)
    pair = arrived[15:]
    mu_next, lam_next = jnp.where(low2, pair, turn(pair, 2)), jnp.where(low2, turn(pair, -2), pair)
    weight = 0.1 * (level_weight * lane_weight)
    muw[4] = turn(jnp.where(low4, mu_next, mu_here[0]), 4) * weight
    lamw[4] = turn(jnp.where(low4, lam_next, lam_here[0]), 4) * weight
    slopes(4, 5)
    strains(0)
    gather_forces()
    send_l[...] = pack_half(f[0].reshape(15, 8, lanes), True)
    send_r[0] = pack_half(f[4].reshape(15, 8, lanes), False)
    copy_l = remote(send_l, recv_l, 2, (left, event))
    copy_l.start()
    copy_r = remote(send_r.at[0], recv_r.at[0], 3, (right, event))
    copy_r.start()

    def advance(place, force):
        for c in range(3):
            rate = b[place, c] - im[place] * force[c]
            b[place, c] = rate
            u[place, c] = u[place, c] + time_step * rate

    for place in (1, 2, 3):
        advance(place, f[place])
        b[place] = b[place] + sm[place]
    slopes(1, 4)
    copy_b.wait_recv()
    later = unpack_half(recv_b[...], 20)
    copy_l.wait_recv()
    from_right = unpack_half(recv_l[...], 15)
    own_last = f[4].reshape(15, 8, lanes)
    full = own_last + turn(from_right, 4)
    heavy = jnp.broadcast_to(later[15:][None], (3, 5, 8, lanes)).reshape(15, 8, lanes)
    u8 = turn(later[:15], 4) - turn(heavy, 4) * full

    def first_force(slot):
        from_left = unpack_half(recv_r[slot], 15)
        mixed = turn(jnp.where(wide, own_last_of(), from_left), 4)
        return (f[0].reshape(15, 8, lanes) + mixed).reshape(3, 5, 8, lanes)

    def own_last_of():
        return f[4].reshape(15, 8, lanes)

    copy_r.wait_recv()
    advance(0, first_force(0))
    b[0] = b[0] + sm[0]
    shared = turn(u[0].reshape(15, 8, lanes), 4)
    u[4] = jnp.where(wide, shared, u8).reshape(3, 5, 8, lanes)
    slopes(0, 1)
    slopes(4, 5)
    strains(1)
    gather_forces()
    send_r[1] = pack_half(f[4].reshape(15, 8, lanes), False)
    copy_s = remote(send_r.at[1], recv_r.at[1], 4, (right, event))
    copy_s.start()

    for i in range(5):
        kacc[i] = middle_sum(kacc[i])
    send_8[...] = kacc[4]
    copy_8 = pltpu.make_async_remote_copy(
        src_ref=send_8,
        dst_ref=recv_8.at[event],
        send_sem=sems.at[0, 5],
        recv_sem=sems_8.at[event],
        device_id=(right, 0),
        device_id_type=MESH,
    )
    copy_8.start()
    first_plane = kacc[0] + jnp.where(low4, 0.0, turn(kacc[4], 4))
    nodes = swap_rows((first_plane, kacc[1], kacc[2], kacc[3]))
    for kind in range(2):
        whole = jnp.concatenate([nodes[2 * kind][0:4], nodes[2 * kind + 1]], axis=0)
        for owner in range(events):
            send_k[owner, kind] = whole[:, planes * owner : planes * owner + planes]
    copies = []
    for offset in range(1, events):
        partner = lax.rem(event + offset, events)
        copy = pltpu.make_async_remote_copy(
            src_ref=send_k.at[partner],
            dst_ref=recv_k.at[offset - 1],
            send_sem=sems_k.at[0, offset - 1],
            recv_sem=sems_k.at[1, offset - 1],
            device_id=(region, partner),
            device_id_type=MESH,
        )
        copy.start()
        copies.append(copy)

    for place in (1, 2, 3):
        advance(place, f[place])
    copy_s.wait_recv()
    advance(0, first_force(1))

    def give(state, forward_out, adjoint_out):
        for c in range(3):
            four = swap_rows((state[0, c], state[1, c], state[2, c], state[3, c]))
            forward_out[c] = jnp.concatenate([four[0][0:4], four[1]], axis=0)
            adjoint_out[c] = jnp.concatenate([four[2][0:4], four[3]], axis=0)

    give(u, uf_out, ua_out)
    give(b, vf_out, va_out)

    total = send_k[event]
    for offset in range(1, events):
        copies[offset - 1].wait_recv()
        total = total + recv_k[offset - 1]
    k_out[...] = total

    @pl.when(event == 0)
    def _():
        extra = None
        for other in range(events):
            pltpu.make_async_copy(recv_8.at[other], recv_8.at[other], sems_8.at[other]).wait()
            extra = recv_8[other] if extra is None else extra + recv_8[other]
        extra = jnp.where(low4, turn(extra, 4), 0.0)
        nothing = jnp.zeros_like(extra)
        parts = swap_rows((extra, nothing, nothing, nothing))
        for kind in range(2):
            whole = jnp.concatenate([parts[2 * kind][0:4], parts[2 * kind + 1]], axis=0)
            k_out[kind] = k_out[kind] + whole[:, 0:planes]

    for copy in [copy_a, copy_b, copy_l, copy_r, copy_s, copy_8] + copies:
        copy.wait_send()


def flush(*refs):
    sources, outs, held, sems = refs[:5], refs[5:10], refs[10:15], refs[15]
    loads = [pltpu.make_async_copy(sources[n], held[n], sems.at[0, n]) for n in range(5)]
    stores = [pltpu.make_async_copy(held[n], outs[n], sems.at[1, n]) for n in range(5)]
    for load in loads:
        load.start()
    for load, store in zip(loads, stores):
        load.wait()
        store.start()
    for store in stores:
        store.wait()


def run(regions, events, interpret, *arrays):
    lanes = arrays[0].shape[-1]
    fields = [jnp.transpose(array[0], (0, 2, 1, 3)) for array in arrays[:5]]
    models = [jnp.transpose(array, (1, 0, 2)) for array in arrays[5:]]
    tables = [jnp.asarray(table) for table in lane_tables(lanes)]
    operands = [*fields, *models, *tables]
    planes = 8 // events
    state = jax.ShapeDtypeStruct((3, 9, 8, lanes), jnp.float32)
    f32 = jnp.float32
    vector = pltpu.VMEM((5, 3, 5, 8, lanes), f32)
    wide = pltpu.VMEM((5, 3, 5, 8, 2 * lanes), f32)
    scalar = pltpu.VMEM((5, 5, 8, lanes), f32)

    def packed(*lead):
        return pltpu.VMEM(lead + (8, lanes), f32)

    outs = pl.pallas_call(
        functools.partial(kernel, regions, events),
        out_shape=[state] * 4 + [jax.ShapeDtypeStruct((2, 9, planes, lanes), f32)],
        in_specs=[pl.BlockSpec(memory_space=pltpu.HBM)] * 12,
        out_specs=[pl.BlockSpec(memory_space=pltpu.VMEM)] * 5,
        scratch_shapes=[
            vector,
            vector,
            vector,
            scalar,
            scalar,
            scalar,
            wide,
            vector,
            wide,
            vector,
            packed(15),
            scalar,
            packed(10),
            packed(10),
            packed(10),
            packed(10),
            packed(8),
            packed(8),
            packed(2, 8),
            packed(2, 8),
            packed(5),
            packed(events, 5),
            pltpu.VMEM((events, 2, 9, planes, lanes), f32),
            pltpu.VMEM((max(events - 1, 1), 2, 9, planes, lanes), f32),
            pltpu.SemaphoreType.DMA((2, 6)),
            pltpu.SemaphoreType.DMA((events,)),
            pltpu.SemaphoreType.DMA((2, max(events - 1, 1))),
            *[pltpu.VMEM(array.shape, array.dtype) for array in operands],
            pltpu.SemaphoreType.DMA((len(operands),)),
        ],
        compiler_params=pltpu.CompilerParams(
            collective_id=0, has_side_effects=True, vmem_limit_bytes=63 * 1024 * 1024
        ),
        name="adjoint_steps",
    )(*operands)
    shapes = [jax.ShapeDtypeStruct(out.shape, out.dtype) for out in outs]
    outs = pl.pallas_call(
        flush,
        out_shape=shapes,
        in_specs=[pl.BlockSpec(memory_space=pltpu.HBM)] * 5,
        out_specs=[pl.BlockSpec(memory_space=pltpu.HBM)] * 5,
        scratch_shapes=[
            *[pltpu.VMEM(shape.shape, shape.dtype) for shape in shapes],
            pltpu.SemaphoreType.DMA((2, 5)),
        ],
        compiler_params=pltpu.CompilerParams(vmem_limit_bytes=63 * 1024 * 1024),
        name="write_out",
    )(*outs)
    forward, forward_rate, adjoint, adjoint_rate = [
        jnp.transpose(out, (0, 2, 1, 3))[None] for out in outs[:4]
    ]
    return (forward, forward_rate, adjoint, adjoint_rate, jnp.transpose(outs[4], (0, 2, 1, 3)))


def solution(mesh):
    field = P("event", None, "region", None, None)
    model = P("region", None, None)
    regions, events = mesh.shape["region"], mesh.shape["event"]
    return jax.shard_map(
        functools.partial(run, regions, events, False),
        mesh=mesh,
        in_specs=(field,) * 5 + (model,) * 3,
        out_specs=(field,) * 4 + (P(None, ("region", "event"), None, None),),
        check_vma=False,
    )
```

```python
import functools
import math

import jax
import jax.numpy as jnp
import numpy as np
from jax import lax
from jax.experimental import pallas as pl
from jax.experimental.pallas import tpu as pltpu
from jax.sharding import PartitionSpec as P

STEPS = 2
time_step = 0.02
MESH = pl.DeviceIdType.MESH


def gll_numbers():
    points = np.array([-1.0, -math.sqrt(3.0 / 7.0), 0.0, math.sqrt(3.0 / 7.0), 1.0])
    weights = np.array([0.1, 49.0 / 90.0, 32.0 / 45.0, 49.0 / 90.0, 0.1])
    legendre = (35.0 * points**4 - 30.0 * points**2 + 3.0) / 8.0
    derivative = np.zeros((5, 5))
    for target in range(5):
        for column in range(5):
            if target != column:
                derivative[target, column] = legendre[target] / (
                    legendre[column] * (points[target] - points[column])
                )
    derivative[0, 0] = -5.0
    derivative[4, 4] = 5.0
    return (derivative, weights)


def lane_tables(lanes):
    numbers, _ = gll_numbers()
    table = np.zeros((lanes, 2 * lanes))
    for lane in range(lanes):
        start, local = lane - lane % 4, lane % 4
        for source in range(5):
            if local:
                table[(start + source) % lanes, lane] += numbers[local, source]
            else:
                right, left = (start + source) % lanes, (start - 4 + source) % lanes
                table[right, lane] += 0.5 * numbers[0, source]
                table[left, lane] += 0.5 * numbers[4, source]
                table[right, lanes + lane] += 0.5 * numbers[0, source]
                table[left, lanes + lane] -= 0.5 * numbers[4, source]
    high = table.astype(np.float32).astype(jnp.bfloat16)
    low = (table - high.astype(np.float64)).astype(np.float32).astype(jnp.bfloat16)
    return (
        np.concatenate([high, high], axis=0),
        low,
        np.concatenate([high.T, low.T], axis=1),
        np.ascontiguousarray(high.T),
    )


def combine(coefficients, pieces):
    total = None
    for number, piece in zip(coefficients, pieces):
        if number != 0.0:
            term = float(number) * piece
            total = term if total is None else total + term
    return total


def turn(value, shift):
    return pltpu.roll(value, shift % 8, value.ndim - 2)


def row_bit(shape, bit):
    return (lax.broadcasted_iota(jnp.int32, shape, len(shape) - 2) & bit) == 0


def swap_rows(four):
    shape = four[0].shape
    low_two, low_one = row_bit(shape, 2), row_bit(shape, 1)
    a0, a1, a2, a3 = four
    b0 = jnp.where(low_two, a0, turn(a2, 2))
    b2 = jnp.where(low_two, turn(a0, -2), a2)
    b1 = jnp.where(low_two, a1, turn(a3, 2))
    b3 = jnp.where(low_two, turn(a1, -2), a3)
    return (
        jnp.where(low_one, b0, turn(b1, 1)),
        jnp.where(low_one, turn(b0, -1), b1),
        jnp.where(low_one, b2, turn(b3, 1)),
        jnp.where(low_one, turn(b2, -1), b3),
    )


def middle_sum(blocks):
    first, last = blocks[..., 0, :, :], blocks[..., 4, :, :]
    low = row_bit(first.shape, 1)
    new_last = last + jnp.where(low, turn(first, -1), 0.0)
    new_first = first + jnp.where(low, 0.0, turn(last, 1))
    return jnp.concatenate(
        [new_first[..., None, :, :], blocks[..., 1:4, :, :], new_last[..., None, :, :]], axis=-3
    )


def pack_half(blocks, low):
    half = (blocks.shape[0] + 1) // 2
    first, second = blocks[:half], blocks[half:]
    if second.shape[0] < half:
        second = jnp.concatenate([second, first[-1:]], axis=0)
    keep = row_bit(first.shape, 4)
    other = turn(second, 4)
    return jnp.where(keep, first, other) if low else jnp.where(keep, other, first)


def unpack_half(packed, count):
    return jnp.concatenate([packed, turn(packed, 4)], axis=0)[:count]


def kernel(
    regions,
    events,
    uf_in,
    vf_in,
    ua_in,
    va_in,
    source_in,
    lam_in,
    mu_in,
    rho_in,
    slope_two_in,
    slope_low_in,
    back_two_in,
    back_high_in,
    uf_out,
    vf_out,
    ua_out,
    va_out,
    k_out,
    u,
    b,
    sm,
    im,
    muw,
    lamw,
    gy,
    sx,
    sy,
    f,
    w8,
    kacc,
    send_a,
    recv_a,
    send_b,
    recv_b,
    send_l,
    recv_l,
    send_r,
    recv_r,
    send_8,
    recv_8,
    send_k,
    recv_k,
    sems,
    sems_8,
    sems_k,
    uf,
    vf,
    ua,
    va,
    source,
    lam,
    mu,
    rho,
    slope_two,
    slope_low,
    back_two,
    back_high,
    load_sems,
):
    numbers, weights = gll_numbers()
    lanes = u.shape[-1]
    region, event = lax.axis_index("region"), lax.axis_index("event")
    left, right = lax.rem(region + regions - 1, regions), lax.rem(region + 1, regions)
    planes = 8 // events

    barrier = pltpu.get_barrier_semaphore()
    for other in range(events):
        for side in (left, right):
            pl.semaphore_signal(barrier, inc=1, device_id=(side, other), device_id_type=MESH)
    for offset in range(1, events):
        partner = lax.rem(event + offset, events)
        pl.semaphore_signal(barrier, inc=1, device_id=(region, partner), device_id_type=MESH)

    loads = {}
    for number, (name, src, dst) in enumerate(
        (
            ("uf", uf_in, uf),
            ("ua", ua_in, ua),
            ("lam", lam_in, lam),
            ("mu", mu_in, mu),
            ("rho", rho_in, rho),
            ("vf", vf_in, vf),
            ("va", va_in, va),
            ("source", source_in, source),
            ("slope_two", slope_two_in, slope_two),
            ("slope_low", slope_low_in, slope_low),
            ("back_two", back_two_in, back_two),
            ("back_high", back_high_in, back_high),
        )
    ):
        loads[name] = pltpu.make_async_copy(src, dst, load_sems.at[number])
        loads[name].start()

    def ready(*names):
        for name in names:
            loads[name].wait()

    def remote(src, dst, number, target):
        return pltpu.make_async_remote_copy(
            src_ref=src,
            dst_ref=dst,
            send_sem=sems.at[0, number],
            recv_sem=sems.at[1, number],
            device_id=target,
            device_id_type=MESH,
        )

    one = (5, 8, lanes)
    low4, low2, low1 = row_bit(one, 4), row_bit(one, 2), row_bit(one, 1)
    lane_place = lax.broadcasted_iota(jnp.int32, one, 2) & 3
    lane_weight = jnp.where(
        lane_place == 0, 0.2, jnp.where(lane_place == 2, 32.0 / 45.0, 49.0 / 90.0)
    ).astype(jnp.float32)
    level = lax.broadcasted_iota(jnp.int32, one, 0)
    edge = (level == 0) | (level == 4)
    inner = jnp.where(level == 2, 32.0 / 45.0, 49.0 / 90.0)
    level_weight = jnp.where(edge, 0.1, inner).astype(jnp.float32)
    closed = ((level == 0) & low1) | ((level == 4) & jnp.logical_not(low1))
    node_weight = jnp.where(edge, jnp.where(closed, 0.1, 0.2), inner).astype(jnp.float32)

    def take(first, second):
        return swap_rows((first[0:5], first[4:9], second[0:5], second[4:9]))

    ready("uf", "ua")
    for comp in range(3):
        for place, value in enumerate(take(uf[comp], ua[comp])):
            u[place, comp] = value
    ready("lam", "mu")
    lam_here, mu_here = take(lam[...], lam[...]), take(mu[...], mu[...])
    edge_pair = jnp.where(low2, mu_here[0], lam_here[0])
    send_a[...] = pack_half(
        jnp.concatenate([u[0].reshape(15, 8, lanes), edge_pair], axis=0), True
    )
    pl.semaphore_wait(barrier, 2 * events + events - 1)
    copy_a = remote(send_a, recv_a, 0, (left, event))
    copy_a.start()

    ready("rho")
    rho_here = take(rho[...], rho[...])
    for place in range(4):
        weight = 0.2 if place == 0 else float(weights[place])
        im[place] = time_step / (rho_here[place] * (weight * (node_weight * lane_weight)))
    ready("vf", "va", "source")
    for comp in range(3):
        rates = take(vf[comp], va[comp])
        sources = take(jnp.zeros_like(source[comp]), source[comp])
        for place in range(4):
            pushed = sources[place] * im[place]
            sm[place, comp] = pushed
            b[place, comp] = rates[place] + pushed
    ahead = u[0] + time_step * b[0]
    send_b[...] = pack_half(
        jnp.concatenate([ahead.reshape(15, 8, lanes), time_step * im[0]], axis=0), True
    )
    copy_b = remote(send_b, recv_b, 1, (left, event))
    copy_b.start()

    for place in range(4):
        weight = float(weights[place]) * (level_weight * lane_weight)
        muw[place] = mu_here[place] * weight
        lamw[place] = lam_here[place] * weight

    def slopes(begin, end):
        rows = (end - begin) * 120
        values = u[begin:end].reshape(rows, lanes)
        high = values.astype(jnp.bfloat16)
        low = (values - high.astype(jnp.float32)).astype(jnp.bfloat16)
        found = jnp.dot(
            jnp.concatenate([high, low], axis=1), slope_two[...], preferred_element_type=jnp.float32
        ) + jnp.dot(high, slope_low[...], preferred_element_type=jnp.float32)
        gy[begin:end] = found.reshape(end - begin, 3, 5, 8, 2 * lanes)

    def strains(step):
        for i in range(5):
            gx = [combine(numbers[i], [u[q, c] for q in range(5)]) for c in range(3)]
            gz = []
            for c in range(3):
                levels = [u[i, c, q] for q in range(5)]
                gz.append(jnp.stack([combine(numbers[k], levels) for k in range(5)]))
            gm = [gy[i, c, :, :, :lanes] for c in range(3)]
            gd = [gy[i, c, :, :, lanes:] for c in range(3)]
            m, l = muw[i], lamw[i]
            xz, xy, zy = gx[1] + gz[0], gx[2] + gm[0], gz[2] + gm[1]
            dilation = gx[0] + gz[1] + gm[2]
            both = m + m
            press = l * dilation
            s_xz, s_xy, s_zy = m * xz, m * xy, m * zy
            sx[i, 0] = both * gx[0] + press
            sx[i, 1] = s_xz
            sx[i, 2] = s_xy
            sy[i, 0, :, :, :lanes] = s_xy
            sy[i, 1, :, :, :lanes] = s_zy
            sy[i, 2, :, :, :lanes] = both * gm[2] + press
            sy[i, 0, :, :, lanes:] = m * gd[0]
            sy[i, 1, :, :, lanes:] = m * gd[1]
            sy[i, 2, :, :, lanes:] = (both + l) * gd[2]
            for c, stress in enumerate((s_xz, both * gz[1] + press, s_zy)):
                levels = [stress[q] for q in range(5)]
                f[i, c] = jnp.stack([combine(numbers[:, k], levels) for k in range(5)])

            def product(value):
                return value * turn(value, -2)

            jump = product(gd[2])
            weight = float(weights[i]) * (level_weight * lane_weight)
            k1 = weight * (product(dilation) + jump)
            shear = product(gx[0]) + product(gz[1]) + product(gm[2]) + jump
            cross = product(xz) + product(xy) + product(zy) + product(gd[0]) + product(gd[1])
            k2 = weight * (2.0 * shear + cross)
            both_kinds = jnp.where(low2, k1, turn(k2, 2))
            kacc[i] = both_kinds if step == 0 else kacc[i] + both_kinds

    def gather_forces(*places):
        for i in places:
            values = sy[i].reshape(120, 2 * lanes)
            high = values.astype(jnp.bfloat16)
            low = (values - high.astype(jnp.float32)).astype(jnp.bfloat16)
            first = jnp.dot(high, back_two[...], preferred_element_type=jnp.float32)
            total = first[:, :lanes] + first[:, lanes:]
            total = total + jnp.dot(low, back_high[...], preferred_element_type=jnp.float32)
            total = total.reshape(3, 5, 8, lanes)
            for c in range(3):
                value = f[i, c] + total[c] + combine(numbers[:, i], [sx[p, c] for p in range(5)])
                f[i, c] = middle_sum(value)

    ready("slope_two", "slope_low", "back_two", "back_high")
    slopes(0, 4)
    copy_a.wait_recv()
    arrived = unpack_half(recv_a[...], 20)
    wide = jnp.broadcast_to(row_bit((8, lanes), 4), (15, 8, lanes))
    next_plane = turn(jnp.where(wide, arrived[:15], u[0].reshape(15, 8, lanes)), 4)
    u[4] = next_plane.reshape(3, 5, 8, lanes)
    pair = arrived[15:]
    mu_next, lam_next = jnp.where(low2, pair, turn(pair, 2)), jnp.where(low2, turn(pair, -2), pair)
    weight = 0.1 * (level_weight * lane_weight)
    muw[4] = turn(jnp.where(low4, mu_next, mu_here[0]), 4) * weight
    lamw[4] = turn(jnp.where(low4, lam_next, lam_here[0]), 4) * weight
    slopes(4, 5)
    strains(0)
    gather_forces(4)
    send_r[0] = pack_half(f[4].reshape(15, 8, lanes), False)
    copy_r = remote(send_r.at[0], recv_r.at[0], 3, (right, event))
    copy_r.start()
    gather_forces(0)
    send_l[...] = pack_half(f[0].reshape(15, 8, lanes), True)
    copy_l = remote(send_l, recv_l, 2, (left, event))
    copy_l.start()
    gather_forces(1, 2, 3)

    def advance(place, force):
        for c in range(3):
            rate = b[place, c] - im[place] * force[c]
            b[place, c] = rate
            u[place, c] = u[place, c] + time_step * rate

    for place in (1, 2, 3):
        advance(place, f[place])
        b[place] = b[place] + sm[place]
    slopes(1, 4)
    copy_b.wait_recv()
    later = unpack_half(recv_b[...], 20)
    copy_l.wait_recv()
    from_right = unpack_half(recv_l[...], 15)
    own_last = f[4].reshape(15, 8, lanes)
    full = own_last + turn(from_right, 4)
    heavy = jnp.broadcast_to(later[15:][None], (3, 5, 8, lanes)).reshape(15, 8, lanes)
    u8 = turn(later[:15], 4) - turn(heavy, 4) * full

    def first_force(slot):
        from_left = unpack_half(recv_r[slot], 15)
        mixed = turn(jnp.where(wide, own_last_of(), from_left), 4)
        return (f[0].reshape(15, 8, lanes) + mixed).reshape(3, 5, 8, lanes)

    def own_last_of():
        return f[4].reshape(15, 8, lanes)

    copy_r.wait_recv()
    advance(0, first_force(0))
    b[0] = b[0] + sm[0]
    shared = turn(u[0].reshape(15, 8, lanes), 4)
    u[4] = jnp.where(wide, shared, u8).reshape(3, 5, 8, lanes)
    slopes(0, 1)
    slopes(4, 5)
    strains(1)
    gather_forces(4)
    send_r[1] = pack_half(f[4].reshape(15, 8, lanes), False)
    copy_s = remote(send_r.at[1], recv_r.at[1], 4, (right, event))
    copy_s.start()

    for i in range(5):
        kacc[i] = middle_sum(kacc[i])
    send_8[...] = kacc[4]
    copy_8 = pltpu.make_async_remote_copy(
        src_ref=send_8,
        dst_ref=recv_8.at[event],
        send_sem=sems.at[0, 5],
        recv_sem=sems_8.at[event],
        device_id=(right, 0),
        device_id_type=MESH,
    )
    copy_8.start()
    first_plane = kacc[0] + jnp.where(low4, 0.0, turn(kacc[4], 4))
    nodes = swap_rows((first_plane, kacc[1], kacc[2], kacc[3]))
    for kind in range(2):
        whole = jnp.concatenate([nodes[2 * kind][0:4], nodes[2 * kind + 1]], axis=0)
        for owner in range(events):
            send_k[owner, kind] = whole[:, planes * owner : planes * owner + planes]
    copies = []
    for offset in range(1, events):
        partner = lax.rem(event + offset, events)
        copy = pltpu.make_async_remote_copy(
            src_ref=send_k.at[partner],
            dst_ref=recv_k.at[offset - 1],
            send_sem=sems_k.at[0, offset - 1],
            recv_sem=sems_k.at[1, offset - 1],
            device_id=(region, partner),
            device_id_type=MESH,
        )
        copy.start()
        copies.append(copy)

    gather_forces(0, 1, 2, 3)
    for place in (1, 2, 3):
        advance(place, f[place])
    copy_s.wait_recv()
    advance(0, first_force(1))

    def give(state, forward_out, adjoint_out):
        for c in range(3):
            four = swap_rows((state[0, c], state[1, c], state[2, c], state[3, c]))
            forward_out[c] = jnp.concatenate([four[0][0:4], four[1]], axis=0)
            adjoint_out[c] = jnp.concatenate([four[2][0:4], four[3]], axis=0)

    give(u, uf_out, ua_out)
    give(b, vf_out, va_out)

    total = send_k[event]
    for offset in range(1, events):
        copies[offset - 1].wait_recv()
        total = total + recv_k[offset - 1]
    k_out[...] = total

    @pl.when(event == 0)
    def _():
        extra = None
        for other in range(events):
            pltpu.make_async_copy(recv_8.at[other], recv_8.at[other], sems_8.at[other]).wait()
            extra = recv_8[other] if extra is None else extra + recv_8[other]
        extra = jnp.where(low4, turn(extra, 4), 0.0)
        nothing = jnp.zeros_like(extra)
        parts = swap_rows((extra, nothing, nothing, nothing))
        for kind in range(2):
            whole = jnp.concatenate([parts[2 * kind][0:4], parts[2 * kind + 1]], axis=0)
            k_out[kind] = k_out[kind] + whole[:, 0:planes]

    for copy in [copy_a, copy_b, copy_l, copy_r, copy_s, copy_8] + copies:
        copy.wait_send()


def flush(*refs):
    sources, outs, sems = refs[:5], refs[5:10], refs[10]
    stores = [pltpu.make_async_copy(sources[n], outs[n], sems.at[n]) for n in range(5)]
    for store in stores:
        store.start()
    for store in stores:
        store.wait()


def run(regions, events, interpret, *arrays):
    lanes = arrays[0].shape[-1]
    fields = [jnp.transpose(array[0], (0, 2, 1, 3)) for array in arrays[:5]]
    models = [jnp.transpose(array, (1, 0, 2)) for array in arrays[5:]]
    tables = [jnp.asarray(table) for table in lane_tables(lanes)]
    operands = [*fields, *models, *tables]
    operands = [pltpu.with_memory_space_constraint(array, pltpu.HBM) for array in operands]
    planes = 8 // events
    state = jax.ShapeDtypeStruct((3, 9, 8, lanes), jnp.float32)
    f32 = jnp.float32
    vector = pltpu.VMEM((5, 3, 5, 8, lanes), f32)
    wide = pltpu.VMEM((5, 3, 5, 8, 2 * lanes), f32)
    scalar = pltpu.VMEM((5, 5, 8, lanes), f32)

    def packed(*lead):
        return pltpu.VMEM(lead + (8, lanes), f32)

    outs = pl.pallas_call(
        functools.partial(kernel, regions, events),
        out_shape=[state] * 4 + [jax.ShapeDtypeStruct((2, 9, planes, lanes), f32)],
        in_specs=[pl.BlockSpec(memory_space=pltpu.HBM)] * 12,
        out_specs=[pl.BlockSpec(memory_space=pltpu.VMEM)] * 5,
        scratch_shapes=[
            vector,
            vector,
            vector,
            scalar,
            scalar,
            scalar,
            wide,
            vector,
            wide,
            vector,
            packed(15),
            scalar,
            packed(10),
            packed(10),
            packed(10),
            packed(10),
            packed(8),
            packed(8),
            packed(2, 8),
            packed(2, 8),
            packed(5),
            packed(events, 5),
            pltpu.VMEM((events, 2, 9, planes, lanes), f32),
            pltpu.VMEM((max(events - 1, 1), 2, 9, planes, lanes), f32),
            pltpu.SemaphoreType.DMA((2, 6)),
            pltpu.SemaphoreType.DMA((events,)),
            pltpu.SemaphoreType.DMA((2, max(events - 1, 1))),
            *[pltpu.VMEM(array.shape, array.dtype) for array in operands],
            pltpu.SemaphoreType.DMA((len(operands),)),
        ],
        compiler_params=pltpu.CompilerParams(
            collective_id=0, has_side_effects=True, vmem_limit_bytes=40 * 1024 * 1024
        ),
        name="adjoint_steps",
    )(*operands)
    shapes = [jax.ShapeDtypeStruct(out.shape, out.dtype) for out in outs]
    shapes = [jax.ShapeDtypeStruct(out.shape, out.dtype) for out in outs]
    outs = pl.pallas_call(
        flush,
        out_shape=shapes,
        in_specs=[pl.BlockSpec(memory_space=pltpu.VMEM)] * 5,
        out_specs=[pl.BlockSpec(memory_space=pltpu.HBM)] * 5,
        scratch_shapes=[pltpu.SemaphoreType.DMA((5,))],
        compiler_params=pltpu.CompilerParams(vmem_limit_bytes=16 * 1024 * 1024),
        name="write_out",
    )(*outs)
    forward, forward_rate, adjoint, adjoint_rate = [
        jnp.transpose(out, (0, 2, 1, 3))[None] for out in outs[:4]
    ]
    return (forward, forward_rate, adjoint, adjoint_rate, jnp.transpose(outs[4], (0, 2, 1, 3)))


def solution(mesh):
    field = P("event", None, "region", None, None)
    model = P("region", None, None)
    regions, events = mesh.shape["region"], mesh.shape["event"]
    return jax.shard_map(
        functools.partial(run, regions, events, False),
        mesh=mesh,
        in_specs=(field,) * 5 + (model,) * 3,
        out_specs=(field,) * 4 + (P(None, ("region", "event"), None, None),),
        check_vma=False,
    )
```

```python
import functools
import math

import jax
import jax.numpy as jnp
import numpy as np
from jax import lax
from jax.experimental import pallas as pl
from jax.experimental.pallas import tpu as pltpu
from jax.sharding import PartitionSpec as P

STEPS = 2
time_step = 0.02
MESH = pl.DeviceIdType.MESH


def gll_numbers():
    points = np.array([-1.0, -math.sqrt(3.0 / 7.0), 0.0, math.sqrt(3.0 / 7.0), 1.0])
    weights = np.array([0.1, 49.0 / 90.0, 32.0 / 45.0, 49.0 / 90.0, 0.1])
    legendre = (35.0 * points**4 - 30.0 * points**2 + 3.0) / 8.0
    derivative = np.zeros((5, 5))
    for target in range(5):
        for column in range(5):
            if target != column:
                derivative[target, column] = legendre[target] / (
                    legendre[column] * (points[target] - points[column])
                )
    derivative[0, 0] = -5.0
    derivative[4, 4] = 5.0
    return (derivative, weights)


def lane_tables(lanes):
    numbers, _ = gll_numbers()
    table = np.zeros((lanes, 2 * lanes))
    for lane in range(lanes):
        start, local = lane - lane % 4, lane % 4
        for source in range(5):
            if local:
                table[(start + source) % lanes, lane] += numbers[local, source]
            else:
                right, left = (start + source) % lanes, (start - 4 + source) % lanes
                table[right, lane] += 0.5 * numbers[0, source]
                table[left, lane] += 0.5 * numbers[4, source]
                table[right, lanes + lane] += 0.5 * numbers[0, source]
                table[left, lanes + lane] -= 0.5 * numbers[4, source]
    high = table.astype(np.float32).astype(jnp.bfloat16)
    low = (table - high.astype(np.float64)).astype(np.float32).astype(jnp.bfloat16)
    return (
        np.concatenate([high, high], axis=0),
        low,
        np.concatenate([high.T, low.T], axis=1),
        np.ascontiguousarray(high.T),
    )


def combine(coefficients, pieces):
    total = None
    for number, piece in zip(coefficients, pieces):
        if number != 0.0:
            term = float(number) * piece
            total = term if total is None else total + term
    return total


def turn(value, shift):
    return pltpu.roll(value, shift % 8, value.ndim - 2)


def row_bit(shape, bit):
    return (lax.broadcasted_iota(jnp.int32, shape, len(shape) - 2) & bit) == 0


def swap_rows(four):
    shape = four[0].shape
    low_two, low_one = row_bit(shape, 2), row_bit(shape, 1)
    a0, a1, a2, a3 = four
    b0 = jnp.where(low_two, a0, turn(a2, 2))
    b2 = jnp.where(low_two, turn(a0, -2), a2)
    b1 = jnp.where(low_two, a1, turn(a3, 2))
    b3 = jnp.where(low_two, turn(a1, -2), a3)
    return (
        jnp.where(low_one, b0, turn(b1, 1)),
        jnp.where(low_one, turn(b0, -1), b1),
        jnp.where(low_one, b2, turn(b3, 1)),
        jnp.where(low_one, turn(b2, -1), b3),
    )


def middle_sum(blocks):
    first, last = blocks[..., 0, :, :], blocks[..., 4, :, :]
    low = row_bit(first.shape, 1)
    new_last = last + jnp.where(low, turn(first, -1), 0.0)
    new_first = first + jnp.where(low, 0.0, turn(last, 1))
    return jnp.concatenate(
        [new_first[..., None, :, :], blocks[..., 1:4, :, :], new_last[..., None, :, :]], axis=-3
    )


def pack_half(blocks, low):
    half = (blocks.shape[0] + 1) // 2
    first, second = blocks[:half], blocks[half:]
    if second.shape[0] < half:
        second = jnp.concatenate([second, first[-1:]], axis=0)
    keep = row_bit(first.shape, 4)
    other = turn(second, 4)
    return jnp.where(keep, first, other) if low else jnp.where(keep, other, first)


def unpack_half(packed, count):
    return jnp.concatenate([packed, turn(packed, 4)], axis=0)[:count]


def kernel(
    regions,
    events,
    uf_in,
    vf_in,
    ua_in,
    va_in,
    source_in,
    lam_in,
    mu_in,
    rho_in,
    slope_two_in,
    slope_low_in,
    back_two_in,
    back_high_in,
    uf_out,
    vf_out,
    ua_out,
    va_out,
    k_out,
    u,
    b,
    sm,
    im,
    muw,
    lamw,
    gy,
    sx,
    sy,
    f,
    w8,
    kacc,
    send_a,
    recv_a,
    send_b,
    recv_b,
    send_l,
    recv_l,
    send_r,
    recv_r,
    send_8,
    recv_8,
    send_k,
    recv_k,
    sems,
    sems_8,
    sems_k,
    uf,
    vf,
    ua,
    va,
    source,
    lam,
    mu,
    rho,
    slope_two,
    slope_low,
    back_two,
    back_high,
    load_sems,
):
    numbers, weights = gll_numbers()
    lanes = u.shape[-1]
    region, event = lax.axis_index("region"), lax.axis_index("event")
    left, right = lax.rem(region + regions - 1, regions), lax.rem(region + 1, regions)
    planes = 8 // events

    barrier = pltpu.get_barrier_semaphore()
    for other in range(events):
        for side in (left, right):
            pl.semaphore_signal(barrier, inc=1, device_id=(side, other), device_id_type=MESH)
    for offset in range(1, events):
        partner = lax.rem(event + offset, events)
        pl.semaphore_signal(barrier, inc=1, device_id=(region, partner), device_id_type=MESH)

    loads = {}
    for number, (name, src, dst) in enumerate(
        (
            ("uf", uf_in, uf),
            ("ua", ua_in, ua),
            ("lam", lam_in, lam),
            ("mu", mu_in, mu),
            ("rho", rho_in, rho),
            ("vf", vf_in, vf),
            ("va", va_in, va),
            ("source", source_in, source),
            ("slope_two", slope_two_in, slope_two),
            ("slope_low", slope_low_in, slope_low),
            ("back_two", back_two_in, back_two),
            ("back_high", back_high_in, back_high),
        )
    ):
        loads[name] = pltpu.make_async_copy(src, dst, load_sems.at[number])
        loads[name].start()

    def ready(*names):
        for name in names:
            loads[name].wait()

    def remote(src, dst, number, target):
        return pltpu.make_async_remote_copy(
            src_ref=src,
            dst_ref=dst,
            send_sem=sems.at[0, number],
            recv_sem=sems.at[1, number],
            device_id=target,
            device_id_type=MESH,
        )

    one = (5, 8, lanes)
    low4, low2, low1 = row_bit(one, 4), row_bit(one, 2), row_bit(one, 1)
    lane_place = lax.broadcasted_iota(jnp.int32, one, 2) & 3
    lane_weight = jnp.where(
        lane_place == 0, 0.2, jnp.where(lane_place == 2, 32.0 / 45.0, 49.0 / 90.0)
    ).astype(jnp.float32)
    level = lax.broadcasted_iota(jnp.int32, one, 0)
    edge = (level == 0) | (level == 4)
    inner = jnp.where(level == 2, 32.0 / 45.0, 49.0 / 90.0)
    level_weight = jnp.where(edge, 0.1, inner).astype(jnp.float32)
    closed = ((level == 0) & low1) | ((level == 4) & jnp.logical_not(low1))
    node_weight = jnp.where(edge, jnp.where(closed, 0.1, 0.2), inner).astype(jnp.float32)

    def take(first, second):
        return swap_rows((first[0:5], first[4:9], second[0:5], second[4:9]))

    ready("uf", "ua")
    for comp in range(3):
        for place, value in enumerate(take(uf[comp], ua[comp])):
            u[place, comp] = value
    ready("lam", "mu")
    lam_here, mu_here = take(lam[...], lam[...]), take(mu[...], mu[...])
    edge_pair = jnp.where(low2, mu_here[0], lam_here[0])
    send_a[...] = pack_half(
        jnp.concatenate([u[0].reshape(15, 8, lanes), edge_pair], axis=0), True
    )
    pl.semaphore_wait(barrier, 2 * events + events - 1)
    copy_a = remote(send_a, recv_a, 0, (left, event))
    copy_a.start()

    ready("rho")
    rho_here = take(rho[...], rho[...])
    for place in range(4):
        weight = 0.2 if place == 0 else float(weights[place])
        im[place] = time_step / (rho_here[place] * (weight * (node_weight * lane_weight)))
    ready("vf", "va", "source")
    for comp in range(3):
        rates = take(vf[comp], va[comp])
        sources = take(jnp.zeros_like(source[comp]), source[comp])
        for place in range(4):
            pushed = sources[place] * im[place]
            sm[place, comp] = pushed
            b[place, comp] = rates[place] + pushed
    ahead = u[0] + time_step * b[0]
    send_b[...] = pack_half(
        jnp.concatenate([ahead.reshape(15, 8, lanes), time_step * im[0]], axis=0), True
    )
    copy_b = remote(send_b, recv_b, 1, (left, event))
    copy_b.start()

    for place in range(4):
        weight = float(weights[place]) * (level_weight * lane_weight)
        muw[place] = mu_here[place] * weight
        lamw[place] = lam_here[place] * weight

    def slopes(begin, end):
        rows = (end - begin) * 120
        values = u[begin:end].reshape(rows, lanes)
        high = values.astype(jnp.bfloat16)
        low = (values - high.astype(jnp.float32)).astype(jnp.bfloat16)
        found = jnp.dot(
            jnp.concatenate([high, low], axis=1), slope_two[...], preferred_element_type=jnp.float32
        ) + jnp.dot(high, slope_low[...], preferred_element_type=jnp.float32)
        gy[begin:end] = found.reshape(end - begin, 3, 5, 8, 2 * lanes)

    def strains(step, forces=True, kinds=True):
        for i in range(5):
            gx = [combine(numbers[i], [u[q, c] for q in range(5)]) for c in range(3)]
            gz = []
            for c in range(3):
                levels = [u[i, c, q] for q in range(5)]
                gz.append(jnp.stack([combine(numbers[k], levels) for k in range(5)]))
            gm = [gy[i, c, :, :, :lanes] for c in range(3)]
            gd = [gy[i, c, :, :, lanes:] for c in range(3)]
            m, l = muw[i], lamw[i]
            xz, xy, zy = gx[1] + gz[0], gx[2] + gm[0], gz[2] + gm[1]
            dilation = gx[0] + gz[1] + gm[2]
            if forces:
                both = m + m
                press = l * dilation
                s_xz, s_xy, s_zy = m * xz, m * xy, m * zy
                sx[i, 0] = both * gx[0] + press
                sx[i, 1] = s_xz
                sx[i, 2] = s_xy
                sy[i, 0, :, :, :lanes] = s_xy
                sy[i, 1, :, :, :lanes] = s_zy
                sy[i, 2, :, :, :lanes] = both * gm[2] + press
                sy[i, 0, :, :, lanes:] = m * gd[0]
                sy[i, 1, :, :, lanes:] = m * gd[1]
                sy[i, 2, :, :, lanes:] = (both + l) * gd[2]
                for c, stress in enumerate((s_xz, both * gz[1] + press, s_zy)):
                    levels = [stress[q] for q in range(5)]
                    f[i, c] = jnp.stack([combine(numbers[:, k], levels) for k in range(5)])
            if not kinds:
                continue

            def product(value):
                return value * turn(value, -2)

            jump = product(gd[2])
            weight = float(weights[i]) * (level_weight * lane_weight)
            k1 = weight * (product(dilation) + jump)
            shear = product(gx[0]) + product(gz[1]) + product(gm[2]) + jump
            cross = product(xz) + product(xy) + product(zy) + product(gd[0]) + product(gd[1])
            k2 = weight * (2.0 * shear + cross)
            both_kinds = jnp.where(low2, k1, turn(k2, 2))
            kacc[i] = both_kinds if step == 0 else kacc[i] + both_kinds

    def gather_forces(*places):
        for i in places:
            values = sy[i].reshape(120, 2 * lanes)
            high = values.astype(jnp.bfloat16)
            low = (values - high.astype(jnp.float32)).astype(jnp.bfloat16)
            first = jnp.dot(high, back_two[...], preferred_element_type=jnp.float32)
            total = first[:, :lanes] + first[:, lanes:]
            total = total + jnp.dot(low, back_high[...], preferred_element_type=jnp.float32)
            total = total.reshape(3, 5, 8, lanes)
            for c in range(3):
                value = f[i, c] + total[c] + combine(numbers[:, i], [sx[p, c] for p in range(5)])
                f[i, c] = middle_sum(value)

    ready("slope_two", "slope_low", "back_two", "back_high")
    slopes(0, 4)
    copy_a.wait_recv()
    arrived = unpack_half(recv_a[...], 20)
    wide = jnp.broadcast_to(row_bit((8, lanes), 4), (15, 8, lanes))
    next_plane = turn(jnp.where(wide, arrived[:15], u[0].reshape(15, 8, lanes)), 4)
    u[4] = next_plane.reshape(3, 5, 8, lanes)
    pair = arrived[15:]
    mu_next, lam_next = jnp.where(low2, pair, turn(pair, 2)), jnp.where(low2, turn(pair, -2), pair)
    weight = 0.1 * (level_weight * lane_weight)
    muw[4] = turn(jnp.where(low4, mu_next, mu_here[0]), 4) * weight
    lamw[4] = turn(jnp.where(low4, lam_next, lam_here[0]), 4) * weight
    slopes(4, 5)
    strains(0, kinds=False)
    gather_forces(4)
    send_r[0] = pack_half(f[4].reshape(15, 8, lanes), False)
    copy_r = remote(send_r.at[0], recv_r.at[0], 3, (right, event))
    copy_r.start()
    gather_forces(0)
    send_l[...] = pack_half(f[0].reshape(15, 8, lanes), True)
    copy_l = remote(send_l, recv_l, 2, (left, event))
    copy_l.start()
    strains(0, forces=False)
    gather_forces(1, 2, 3)

    def advance(place, force):
        for c in range(3):
            rate = b[place, c] - im[place] * force[c]
            b[place, c] = rate
            u[place, c] = u[place, c] + time_step * rate

    for place in (1, 2, 3):
        advance(place, f[place])
        b[place] = b[place] + sm[place]
    slopes(1, 4)
    copy_b.wait_recv()
    later = unpack_half(recv_b[...], 20)
    copy_l.wait_recv()
    from_right = unpack_half(recv_l[...], 15)
    own_last = f[4].reshape(15, 8, lanes)
    full = own_last + turn(from_right, 4)
    heavy = jnp.broadcast_to(later[15:][None], (3, 5, 8, lanes)).reshape(15, 8, lanes)
    u8 = turn(later[:15], 4) - turn(heavy, 4) * full

    def first_force(slot):
        from_left = unpack_half(recv_r[slot], 15)
        mixed = turn(jnp.where(wide, own_last_of(), from_left), 4)
        return (f[0].reshape(15, 8, lanes) + mixed).reshape(3, 5, 8, lanes)

    def own_last_of():
        return f[4].reshape(15, 8, lanes)

    copy_r.wait_recv()
    advance(0, first_force(0))
    b[0] = b[0] + sm[0]
    shared = turn(u[0].reshape(15, 8, lanes), 4)
    u[4] = jnp.where(wide, shared, u8).reshape(3, 5, 8, lanes)
    slopes(0, 1)
    slopes(4, 5)
    strains(1)
    gather_forces(4)
    send_r[1] = pack_half(f[4].reshape(15, 8, lanes), False)
    copy_s = remote(send_r.at[1], recv_r.at[1], 4, (right, event))
    copy_s.start()

    for i in range(5):
        kacc[i] = middle_sum(kacc[i])
    send_8[...] = kacc[4]
    copy_8 = pltpu.make_async_remote_copy(
        src_ref=send_8,
        dst_ref=recv_8.at[event],
        send_sem=sems.at[0, 5],
        recv_sem=sems_8.at[event],
        device_id=(right, 0),
        device_id_type=MESH,
    )
    copy_8.start()
    first_plane = kacc[0] + jnp.where(low4, 0.0, turn(kacc[4], 4))
    nodes = swap_rows((first_plane, kacc[1], kacc[2], kacc[3]))
    for kind in range(2):
        whole = jnp.concatenate([nodes[2 * kind][0:4], nodes[2 * kind + 1]], axis=0)
        for owner in range(events):
            send_k[owner, kind] = whole[:, planes * owner : planes * owner + planes]
    copies = []
    for offset in range(1, events):
        partner = lax.rem(event + offset, events)
        copy = pltpu.make_async_remote_copy(
            src_ref=send_k.at[partner],
            dst_ref=recv_k.at[offset - 1],
            send_sem=sems_k.at[0, offset - 1],
            recv_sem=sems_k.at[1, offset - 1],
            device_id=(region, partner),
            device_id_type=MESH,
        )
        copy.start()
        copies.append(copy)

    gather_forces(0, 1, 2, 3)
    for place in (1, 2, 3):
        advance(place, f[place])
    copy_s.wait_recv()
    advance(0, first_force(1))

    def give(state, forward_out, adjoint_out):
        for c in range(3):
            four = swap_rows((state[0, c], state[1, c], state[2, c], state[3, c]))
            forward_out[c] = jnp.concatenate([four[0][0:4], four[1]], axis=0)
            adjoint_out[c] = jnp.concatenate([four[2][0:4], four[3]], axis=0)

    give(u, uf_out, ua_out)
    give(b, vf_out, va_out)

    total = send_k[event]
    for offset in range(1, events):
        copies[offset - 1].wait_recv()
        total = total + recv_k[offset - 1]
    k_out[...] = total

    @pl.when(event == 0)
    def _():
        extra = None
        for other in range(events):
            pltpu.make_async_copy(recv_8.at[other], recv_8.at[other], sems_8.at[other]).wait()
            extra = recv_8[other] if extra is None else extra + recv_8[other]
        extra = jnp.where(low4, turn(extra, 4), 0.0)
        nothing = jnp.zeros_like(extra)
        parts = swap_rows((extra, nothing, nothing, nothing))
        for kind in range(2):
            whole = jnp.concatenate([parts[2 * kind][0:4], parts[2 * kind + 1]], axis=0)
            k_out[kind] = k_out[kind] + whole[:, 0:planes]

    for copy in [copy_a, copy_b, copy_l, copy_r, copy_s, copy_8] + copies:
        copy.wait_send()


def flush(*refs):
    sources, outs, sems = refs[:5], refs[5:10], refs[10]
    stores = [pltpu.make_async_copy(sources[n], outs[n], sems.at[n]) for n in range(5)]
    for store in stores:
        store.start()
    for store in stores:
        store.wait()


def run(regions, events, interpret, *arrays):
    lanes = arrays[0].shape[-1]
    fields = [jnp.transpose(array[0], (0, 2, 1, 3)) for array in arrays[:5]]
    models = [jnp.transpose(array, (1, 0, 2)) for array in arrays[5:]]
    tables = [jnp.asarray(table) for table in lane_tables(lanes)]
    operands = [*fields, *models, *tables]
    operands = [pltpu.with_memory_space_constraint(array, pltpu.HBM) for array in operands]
    planes = 8 // events
    state = jax.ShapeDtypeStruct((3, 9, 8, lanes), jnp.float32)
    f32 = jnp.float32
    vector = pltpu.VMEM((5, 3, 5, 8, lanes), f32)
    wide = pltpu.VMEM((5, 3, 5, 8, 2 * lanes), f32)
    scalar = pltpu.VMEM((5, 5, 8, lanes), f32)

    def packed(*lead):
        return pltpu.VMEM(lead + (8, lanes), f32)

    outs = pl.pallas_call(
        functools.partial(kernel, regions, events),
        out_shape=[state] * 4 + [jax.ShapeDtypeStruct((2, 9, planes, lanes), f32)],
        in_specs=[pl.BlockSpec(memory_space=pltpu.HBM)] * 12,
        out_specs=[pl.BlockSpec(memory_space=pltpu.VMEM)] * 5,
        scratch_shapes=[
            vector,
            vector,
            vector,
            scalar,
            scalar,
            scalar,
            wide,
            vector,
            wide,
            vector,
            packed(15),
            scalar,
            packed(10),
            packed(10),
            packed(10),
            packed(10),
            packed(8),
            packed(8),
            packed(2, 8),
            packed(2, 8),
            packed(5),
            packed(events, 5),
            pltpu.VMEM((events, 2, 9, planes, lanes), f32),
            pltpu.VMEM((max(events - 1, 1), 2, 9, planes, lanes), f32),
            pltpu.SemaphoreType.DMA((2, 6)),
            pltpu.SemaphoreType.DMA((events,)),
            pltpu.SemaphoreType.DMA((2, max(events - 1, 1))),
            *[pltpu.VMEM(array.shape, array.dtype) for array in operands],
            pltpu.SemaphoreType.DMA((len(operands),)),
        ],
        compiler_params=pltpu.CompilerParams(
            collective_id=0, has_side_effects=True, vmem_limit_bytes=40 * 1024 * 1024
        ),
        name="adjoint_steps",
    )(*operands)
    shapes = [jax.ShapeDtypeStruct(out.shape, out.dtype) for out in outs]
    shapes = [jax.ShapeDtypeStruct(out.shape, out.dtype) for out in outs]
    outs = pl.pallas_call(
        flush,
        out_shape=shapes,
        in_specs=[pl.BlockSpec(memory_space=pltpu.VMEM)] * 5,
        out_specs=[pl.BlockSpec(memory_space=pltpu.HBM)] * 5,
        scratch_shapes=[pltpu.SemaphoreType.DMA((5,))],
        compiler_params=pltpu.CompilerParams(vmem_limit_bytes=16 * 1024 * 1024),
        name="write_out",
    )(*outs)
    forward, forward_rate, adjoint, adjoint_rate = [
        jnp.transpose(out, (0, 2, 1, 3))[None] for out in outs[:4]
    ]
    return (forward, forward_rate, adjoint, adjoint_rate, jnp.transpose(outs[4], (0, 2, 1, 3)))


def solution(mesh):
    field = P("event", None, "region", None, None)
    model = P("region", None, None)
    regions, events = mesh.shape["region"], mesh.shape["event"]
    return jax.shard_map(
        functools.partial(run, regions, events, False),
        mesh=mesh,
        in_specs=(field,) * 5 + (model,) * 3,
        out_specs=(field,) * 4 + (P(None, ("region", "event"), None, None),),
        check_vma=False,
    )
```
